256 devices in a mesh: seq: 8 (over y, core), exp: 32 (over x, z).
Axes of the slice: x: 4, y: 4, z: 8, core: 2. Of those that a mesh axis runs over, the one named last changes fastest.
Arguments:
- layer_input: bfloat16 [32, 2048, 2048], P('exp', 'seq'), may hold values from -6 to 6
- queries: bfloat16 [32, 2048, 2048], P('exp', 'seq'), may hold values from -6 to 6
- keys_in: bfloat16 [32, 2048, 2048], P('exp', 'seq'), may hold values from -0.59765625 to 0.59765625
- values_in: bfloat16 [32, 2048, 2048], P('exp', 'seq'), may hold values from -6 to 6
- decay_rate: float32 [32, 2048, 16], P('exp', 'seq'), as said below
- attn_gain: float32 [2048], replicated, may hold values from 0.25 to 1.75
- norm_gain: float32 [2048], replicated, may hold values from 0.25 to 1.75
- expert_ids: int32 [32, 2048, 2], P('exp', 'seq'), may hold values from 0 to 31, all different within a row; in each aligned block of 256 rows (0 to 255, 256 to 511, ..., all dimensions but the last counted through in order) at most 24 rows name the same one
- gate_levels: int32 [32, 2048, 2], P('exp', 'seq'), may hold values from 1 to 256
- w_gate: bfloat16 [32, 2048, 768], P('exp'), may hold values from -0.125 to 0.125
- w_up: bfloat16 [32, 2048, 768], P('exp'), may hold values from -0.125 to 0.125
- w_down: bfloat16 [32, 768, 2048], P('exp'), may hold values from -0.21875 to 0.21875
Outputs:
- layer_out: bfloat16 [32, 2048, 2048], P('exp', 'seq')
The draws below stay inside these ranges and needn't reach their ends.
Inputs may be any that keep to these rules, and one draw needn't show every extreme that they name: `expert_ids`: each token names 2 different experts. Among the 256 positions of one device, no expert is named by more than 24 routes, a bound that some block reaches. `decay_rate`: every entry is positive.
All inputs are finite; a program needn't handle non-finite values.
Results may differ from the reference program's by a relative error of at most 0.01.
Values may be sent and summed in bfloat16 or wider, within the bound.
No kernel may reach another device: no remote copies, remote signals or barrier semaphores. Data moves between devices by JAX's collectives and lax.ppermute only.
A program may use at most 128 MiB of HBM per device.

```python
import math
import jax
import jax.numpy as jnp
import numpy as np
from jax import lax

D = 2048
HEADS = 16
DH = 128
FF = 768
TOP = 2
TOK_DEV = 256
EXPERTS = 32
CAP = 24
SEQUENCE_COUNT = 32
SEQUENCE_LENGTH = 2048
N_SEQ = 8


def draw_decay_rate(key, part):
    random_key_list = jax.random.split(key, 7)
    full_shape = (SEQUENCE_COUNT, SEQUENCE_LENGTH, HEADS)
    fast_share = 0.5
    fast_head = jax.random.uniform(random_key_list[0], (SEQUENCE_COUNT, 1, HEADS)) < fast_share
    slow_total = jax.random.uniform(random_key_list[1], (SEQUENCE_COUNT, 1, HEADS), minval=0.05, maxval=0.25)
    block_count = SEQUENCE_LENGTH // TOK_DEV
    block_factor = 2.0 ** jax.random.uniform(random_key_list[2], (SEQUENCE_COUNT, block_count, HEADS), minval=-1.0, maxval=1.0)
    block_factor = jnp.repeat(block_factor, TOK_DEV, axis=1)
    rough_factor = jax.random.uniform(random_key_list[3], full_shape, minval=0.5, maxval=1.5)
    slow_rate = slow_total / SEQUENCE_LENGTH * block_factor * rough_factor
    fast_rate = rough_factor / jax.random.uniform(random_key_list[4], (SEQUENCE_COUNT, 1, HEADS), minval=30.0, maxval=50.0)
    baseline_rate = jnp.where(fast_head, fast_rate, slow_rate)
    spike_positions = jax.random.randint(random_key_list[5], (SEQUENCE_COUNT, 2), 0, SEQUENCE_LENGTH)
    draw_amount = jax.random.uniform(random_key_list[6], (SEQUENCE_COUNT, 2), minval=0.22, maxval=0.6)
    position_indices = jnp.arange(SEQUENCE_LENGTH)[None, :, None]
    spike_rate = jnp.sum(jnp.where(position_indices == spike_positions[:, None, :], draw_amount[:, None, :], 0.0), axis=2)
    return (baseline_rate + spike_rate[:, :, None]).astype(jnp.float32)


def place_ends(values, rng, least, high):
    shape = values.shape
    place = [jax.random.randint(jax.random.fold_in(rng, axis), (), 0, shape[axis]) for axis in range(len(shape))]
    values = values.at[tuple(place)].set(least)
    longest = shape.index(max(shape))
    place[longest] = (place[longest] + 1) % shape[longest]
    return values.at[tuple(place)].set(high)


def level_of(rng, shape, cuts, least, high):
    loudness, own = 1.0, jax.random.fold_in(rng, 6)
    for axis_at, shards_of in cuts:
        steps = jnp.exp(jax.random.uniform(jax.random.fold_in(own, axis_at), (shards_of,), jnp.float32, least / len(cuts), high / len(cuts)))
        loudness = loudness * jnp.repeat(steps, shape[axis_at] // shards_of).reshape([-1 if axis == axis_at else 1 for axis in range(len(shape))])
    return loudness


def deal_out(rng, own, number, rows, count, top, limit, slope):
    sequence = jax.random.permutation(rng, count)
    heavy_load, usual = shares(count, rows * top, limit, slope, True), shares(count, rows * top, limit, slope, False)
    places = jnp.arange(count)

    def named(lengths, offset_by):
        used = int((lengths > 0).sum())
        fixed = max(1, used // 4)
        passed = fixed + (places - fixed + offset_by * (used - fixed)) % max(1, count - fixed)
        return jnp.zeros((count,), jnp.int32).at[sequence[jnp.where(places < fixed, places, passed)]].set(jnp.asarray(lengths, jnp.int32))

    lengths = jnp.where(number % 4 == 0, named(heavy_load, number // 4), named(usual, number - number // 4 - 1))
    mixed = jax.random.permutation(jax.random.fold_in(own, 3), count)
    source_of, receiver = mixed[0:count // 2 * 2:2], mixed[1:count // 2 * 2:2]
    margin = jnp.minimum(lengths[source_of] - 1, limit - lengths[receiver]) // 2
    margin = jnp.where((source_of == sequence[0]) | (receiver == sequence[0]) | (lengths[receiver] == 0), 0, jnp.maximum(margin, 0))
    passed = jax.random.randint(jax.random.fold_in(own, 4), (count // 2,), 0, 1 << 20) % (margin + 1)
    lengths = lengths.at[source_of].add(-passed).at[receiver].add(passed)
    members = jnp.searchsorted(jnp.cumsum(lengths), jnp.arange(rows * top), side="right").astype(jnp.int32)
    grid = members.reshape(top, rows).T
    grid = grid[jax.random.permutation(jax.random.fold_in(own, 1), rows)]
    offset_by = jax.random.randint(jax.random.fold_in(own, 2), (rows, 1), 0, top)
    return jnp.take_along_axis(grid, (jnp.arange(top)[None, :] + offset_by) % top, axis=1)


def shares(amount, total, most, slope, full):
    weights = [(1 << 20) // math.isqrt(standing ** slope) + 1 for standing in range(1, amount + 1)]
    largest = most if full else min(most, max(-(-total // amount), total * weights[0] // sum(weights)))
    least = 1 if total - largest >= amount - 1 else 0
    holding, rest = [largest] + [least] * (amount - 1), total - largest - least * (amount - 1)
    while rest > 0:
        movable = [i for i in range(1, amount) if holding[i] < largest] or [i for i in range(1, amount) if holding[i] < most]
        whole, budget = sum([weights[i] for i in movable]), rest
        for i in movable:
            more = min(most - holding[i], max(1, budget * weights[i] // whole), rest)
            holding[i] = holding[i] + more
            rest = rest - more
    return np.array(holding)


def noise(key, dims, spread, limit, shards=(), kind=jnp.bfloat16):
    entries = spread * jax.random.normal(key, dims, jnp.float32)
    if shards:
        entries = entries * level_of(key, dims, shards, -0.22, 0.18)
    return jnp.clip(entries, -limit, limit).astype(kind)


def setup_inputs(seed: int = 0) -> dict:
    seeds = jax.random.split(jax.random.key(seed), 13)
    layer_input = noise(seeds[0], (SEQUENCE_COUNT, SEQUENCE_LENGTH, D), 1.0, 6.0, ((0, 32), (1, 8)))
    queries = noise(seeds[1], (SEQUENCE_COUNT, SEQUENCE_LENGTH, D), 1.0, 6.0, ((0, 32), (1, 8)))
    keys_in = noise(seeds[2], (SEQUENCE_COUNT, SEQUENCE_LENGTH, D), 0.0884, 0.59765625, ((0, 32), (1, 8)))
    values_in = noise(seeds[3], (SEQUENCE_COUNT, SEQUENCE_LENGTH, D), 1.0, 6.0, ((0, 32), (1, 8)))
    decay_rate = draw_decay_rate(jax.random.fold_in(seeds[12], 71), 0)
    attn_gain = jnp.clip(1.0 + 0.15 * jax.random.normal(seeds[5], (D,), jnp.float32), 0.25, 1.75)
    norm_gain = jnp.clip(1.0 + 0.15 * jax.random.normal(seeds[6], (D,), jnp.float32), 0.25, 1.75)
    expert_ids_keys = jax.random.split(jax.random.fold_in(seeds[7], 1), SEQUENCE_COUNT * SEQUENCE_LENGTH // TOK_DEV)
    expert_ids_turns = jax.random.permutation(jax.random.fold_in(seeds[7], 3), SEQUENCE_COUNT * SEQUENCE_LENGTH // TOK_DEV)
    expert_ids = jax.vmap(lambda own, number: deal_out(jax.random.fold_in(seeds[7], 2), own, number, TOK_DEV, EXPERTS, TOP, CAP, 1))(expert_ids_keys, expert_ids_turns).reshape((SEQUENCE_COUNT, SEQUENCE_LENGTH, TOP))
    gate_levels = place_ends(jax.random.randint(seeds[8], (SEQUENCE_COUNT, SEQUENCE_LENGTH, TOP), 1, 257), jax.random.fold_in(seeds[8], 1), 1, 256).astype(jnp.int32)
    w_gate = noise(seeds[9], (EXPERTS, D, FF), D ** -0.5, 0.125, ((0, 32),))
    w_up = noise(seeds[10], (EXPERTS, D, FF), D ** -0.5, 0.125, ((0, 32),))
    w_down = noise(seeds[11], (EXPERTS, FF, D), FF ** -0.5, 0.21875, ((0, 32),))
    return dict(layer_input=layer_input, queries=queries, keys_in=keys_in, values_in=values_in, decay_rate=decay_rate, attn_gain=attn_gain, norm_gain=norm_gain, expert_ids=expert_ids, gate_levels=gate_levels, w_gate=w_gate, w_up=w_up, w_down=w_down)


def attend_block(carried, block_data):
    query_block, key_block, value_block, decay_block = block_data
    block_len = query_block.shape[0]
    cumulative = -jnp.cumsum(decay_block, axis=0)
    block_total = cumulative[-1]
    query_heads = query_block.reshape(block_len, HEADS, DH).astype(jnp.float32)
    key_heads = key_block.reshape(block_len, HEADS, DH).astype(jnp.float32)
    value_heads = value_block.reshape(block_len, HEADS, DH).astype(jnp.float32)
    scores = jnp.einsum('thd,shd->hts', query_heads, key_heads)
    cum_heads = cumulative.T
    log_gap = cum_heads[:, :, None] - cum_heads[:, None, :]
    row_index = jnp.arange(block_len)[:, None]
    col_index = jnp.arange(block_len)[None, :]
    causal = (row_index >= col_index)[None]
    weights = jnp.where(causal, jnp.exp(jnp.minimum(log_gap, 0.0)), 0.0)
    attn_probs = (scores * weights).astype(jnp.bfloat16)
    intra_part = jnp.einsum('hts,shd->thd', attn_probs.astype(jnp.float32), value_heads)
    inter_part = jnp.exp(cumulative)[:, :, None] * jnp.einsum('thd,hde->the', query_heads, carried, precision=lax.Precision.HIGHEST)
    key_weighted = key_heads * jnp.exp(block_total[None, :] - cumulative)[:, :, None]
    contrib = jnp.einsum('thd,the->hde', key_weighted, value_heads, precision=lax.Precision.HIGHEST)
    new_state = jnp.exp(block_total)[:, None, None] * carried + contrib
    return (new_state, intra_part + inter_part)

def one_sequence(seq_args):
    seq_query, seq_keys, seq_values, seq_decay = seq_args
    blocks = (seq_query.reshape(N_SEQ, TOK_DEV, D), seq_keys.reshape(N_SEQ, TOK_DEV, D), seq_values.reshape(N_SEQ, TOK_DEV, D), seq_decay.reshape(N_SEQ, TOK_DEV, HEADS))
    zero_state = jnp.zeros((HEADS, DH, DH), jnp.float32)
    final_state, outputs = lax.scan(attend_block, zero_state, blocks)
    return outputs.reshape(SEQUENCE_LENGTH, HEADS, DH)

def reference(layer_input, queries, keys_in, values_in, decay_rate, attn_gain, norm_gain, expert_ids, gate_levels, w_gate, w_up, w_down):
    raw_attn = lax.map(one_sequence, (queries, keys_in, values_in, decay_rate))
    normed_heads = raw_attn / jnp.sqrt(lax.optimization_barrier(jnp.mean(raw_attn * raw_attn, axis=-1, keepdims=True)) + 1e-06)
    h_res = layer_input.astype(jnp.float32) + normed_heads.reshape(SEQUENCE_COUNT, SEQUENCE_LENGTH, D) * attn_gain
    normed = (norm_gain * h_res / jnp.sqrt(lax.optimization_barrier(jnp.mean(h_res * h_res, axis=-1, keepdims=True)) + 1e-06)).astype(jnp.bfloat16)
    row_count = SEQUENCE_COUNT * SEQUENCE_LENGTH
    routed = jnp.repeat(normed.reshape(row_count, D), TOP, axis=0)
    flat_ids = expert_ids.reshape(-1).astype(jnp.int32)
    gate_scale = gate_levels.reshape(-1).astype(jnp.float32) / 256.0
    slots_total = SEQUENCE_COUNT * N_SEQ * CAP

    def per_expert(accum_out, expert_item):
        expert, weight_gate, weight_up, weight_down = expert_item
        chosen = flat_ids == expert
        position = jnp.cumsum(chosen.astype(jnp.int32)) - 1
        slot_index = jnp.where(chosen, position, slots_total).astype(jnp.int32)
        buffer = jnp.zeros((slots_total, D), jnp.bfloat16).at[slot_index].set(routed, mode='drop')
        gate_part = jnp.dot(buffer, weight_gate, preferred_element_type=jnp.float32)
        up_part = jnp.dot(buffer, weight_up, preferred_element_type=jnp.float32)
        activation = (jax.nn.silu(gate_part) * up_part).astype(jnp.bfloat16)
        result = jnp.dot(activation, weight_down, preferred_element_type=jnp.float32).astype(jnp.bfloat16)
        picked = result[jnp.minimum(slot_index, slots_total - 1)].astype(jnp.float32)
        accum_out = accum_out + jnp.where(chosen, gate_scale, 0.0)[:, None] * picked
        return (accum_out, None)
    zero_out = jnp.zeros((row_count * TOP, D), jnp.float32)
    accum_out, unused = lax.scan(per_expert, zero_out, (jnp.arange(EXPERTS, dtype=jnp.int32), w_gate, w_up, w_down))
    moe_out = lax.optimization_barrier(jnp.sum(accum_out.reshape(row_count, TOP, D), axis=1))
    return (h_res + moe_out.reshape(SEQUENCE_COUNT, SEQUENCE_LENGTH, D)).astype(jnp.bfloat16)
```

```python
import jax
import jax.numpy as jnp
from jax import lax
from jax.experimental import pallas as pl
from jax.experimental.pallas import tpu as pltpu
from jax.sharding import PartitionSpec as P

F32 = jnp.float32
BF16 = jnp.bfloat16
EXACT = lax.Precision.HIGHEST
VMEM_LIMIT = 56 * 1024 * 1024
LOG_ROWS = 16


def call(body, out_shape, **kw):
    return pl.pallas_call(
        body,
        out_shape=out_shape,
        compiler_params=pltpu.CompilerParams(vmem_limit_bytes=VMEM_LIMIT),
        **kw,
    )


def dot(a, b, ca=1, cb=0, precision=None):
    return lax.dot_general(
        a, b, (((ca,), (cb,)), ((), ())), precision=precision, preferred_element_type=F32
    )


def iota(shape, dim):
    return lax.broadcasted_iota(jnp.int32, shape, dim)


def contrib_body(k_ref, v_ref, decay_ref, out_ref, cum_ref, cum_t_ref):
    block, heads = decay_ref.shape
    groups = out_ref.shape[0]
    per = heads // groups
    dh = k_ref.shape[1] // heads
    lower = (iota((block, block), 0) >= iota((block, block), 1)).astype(F32)
    decay = decay_ref[...]
    cum = -dot(lower, decay, precision=EXACT)
    cum_t = -dot(decay, lower, 0, 1, precision=EXACT)
    cum_ref[...] = cum
    cum_t_ref[...] = cum_t
    total = cum[block - 1 : block, :]
    decayed = jnp.exp(total - cum)
    for g in range(groups):
        row = iota((LOG_ROWS, dh), 0)
        logs = jnp.zeros((LOG_ROWS, dh), F32)
        for i in range(per):
            h = g * per + i
            cols = slice(h * dh, (h + 1) * dh)
            kw = (k_ref[:, cols].astype(F32) * decayed[:, h : h + 1]).astype(BF16)
            out_ref[g, i * dh : (i + 1) * dh, :] = dot(kw, v_ref[:, cols], 0, 0).astype(BF16)
            rest = jnp.broadcast_to(total[:, h : h + 1], (LOG_ROWS, dh))
            for piece in range(3):
                part = rest.astype(BF16).astype(F32)
                logs = jnp.where(row == 3 * i + piece, part, logs)
                rest = rest - part
        out_ref[g, per * dh :, :] = logs.astype(BF16)


def prefix_body(x_ref, out_ref):
    blocks, rows, dh = out_ref.shape
    per = rows // dh
    for i in range(per):
        here = slice(i * dh, (i + 1) * dh)
        state = jnp.zeros((dh, dh), F32)
        for b in range(blocks):
            out_ref[b, here, :] = state.astype(BF16)
            pieces = [
                x_ref[b, rows + 3 * i + p : rows + 3 * i + p + 1, :].astype(F32) for p in range(3)
            ]
            state = jnp.exp(pieces[0] + pieces[1] + pieces[2]) * state + x_ref[b, here, :].astype(F32)


def intra_body(q_ref, k_ref, v_ref, cum_ref, cum_t_ref, out_ref):
    block, heads = cum_ref.shape
    dh = q_ref.shape[1] // heads
    half = block // 2
    cum = cum_ref[...]
    cum_t = cum_t_ref[...]
    for h in range(heads):
        cols = slice(h * dh, (h + 1) * dh)
        for lo, hi in ((0, half), (half, block)):
            scores = dot(q_ref[lo:hi, cols], k_ref[:hi, cols], 1, 1)
            gap = cum[lo:hi, h : h + 1] - cum_t[h : h + 1, :hi]
            seen = iota((hi - lo, hi), 0) + lo >= iota((hi - lo, hi), 1)
            probs = jnp.where(seen, scores * jnp.exp(jnp.minimum(gap, 0.0)), 0.0).astype(BF16)
            out_ref[lo:hi, cols] = dot(probs, v_ref[:hi, cols])


def finish_body(
    intra_ref, q_ref, carried_ref, cum_ref, x_ref, attn_gain_ref, norm_gain_ref, ids_ref, h_ref, send_ref, normed_ref
):
    block, heads = cum_ref.shape
    width = q_ref.shape[1]
    dh = width // heads
    per = carried_ref.shape[1] // dh
    grow = jnp.exp(cum_ref[...])
    squares = jnp.zeros((block, dh), F32)
    for h in range(heads):
        cols = slice(h * dh, (h + 1) * dh)
        state = carried_ref[h // per, (h % per) * dh : (h % per + 1) * dh, :]
        raw = intra_ref[:, cols] + grow[:, h : h + 1] * dot(q_ref[:, cols], state)
        scale = lax.rsqrt(jnp.mean(raw * raw, axis=-1, keepdims=True) + 1e-06)
        res = x_ref[:, cols].astype(F32) + attn_gain_ref[:, cols] * (raw * scale)
        h_ref[:, cols] = res
        squares = squares + res * res
    scale = lax.rsqrt(jnp.sum(squares, axis=-1, keepdims=True) / width + 1e-06)
    for h in range(heads):
        cols = slice(h * dh, (h + 1) * dh)
        normed_ref[:, cols] = (norm_gain_ref[:, cols] * h_ref[:, cols] * scale).astype(BF16)
    slots = send_ref.shape[0]
    experts = slots // (3 * block // 32)
    cap = slots // experts
    expert = iota((experts, block), 0)
    member = (ids_ref[0:1, :] == expert) | (ids_ref[1:2, :] == expert)
    member = member.astype(F32)
    earlier = (iota((block, block), 0) < iota((block, block), 1)).astype(BF16)
    rank = (dot(member.astype(BF16), earlier) + 1.0) * member
    spread = (iota((slots, experts), 0) // cap == iota((slots, experts), 1)).astype(BF16)
    ranks = dot(spread, rank.astype(BF16))
    wanted = (iota((slots, block), 0) % cap + 1).astype(F32)
    pick = (ranks == wanted).astype(BF16)
    step = 512
    for c in range(0, width, step):
        send_ref[:, c : c + step] = dot(pick, normed_ref[:, c : c + step]).astype(BF16)


def expert_body(x_ref, gate_ref, up_ref, down_ref, out_ref, act_ref, *, hidden_steps, hidden_block):
    i = pl.program_id(0)
    for j in range(hidden_steps):

        @pl.when(i == j)
        def _():
            x = x_ref[...]
            gate = dot(x, gate_ref[...])
            up = dot(x, up_ref[...])
            act_ref[:, j * hidden_block : (j + 1) * hidden_block] = (
                gate / (1.0 + jnp.exp(-gate)) * up
            ).astype(BF16)

    @pl.when(i >= hidden_steps)
    def _():
        out_ref[...] = dot(act_ref[...], down_ref[...]).astype(BF16)


def combine_body(back_ref, h_ref, ids_ref, levels_ref, out_ref, mix_ref):
    block = h_ref.shape[0]
    slots = back_ref.shape[0]

    @pl.when(pl.program_id(0) == 0)
    def _():
        experts = slots // (3 * block // 32)
        cap = slots // experts
        expert = iota((block, experts), 1)
        first = ids_ref[:, 0:1] == expert
        second = ids_ref[:, 1:2] == expert
        member = (first | second).astype(F32)
        later = (iota((block, block), 0) > iota((block, block), 1)).astype(BF16)
        rank = (dot(later, member.astype(BF16)) + 1.0) * member
        level = jnp.where(first, levels_ref[:, 0:1], 0) + jnp.where(second, levels_ref[:, 1:2], 0)
        spread = (iota((experts, slots), 1) // cap == iota((experts, slots), 0)).astype(BF16)
        ranks = dot(rank.astype(BF16), spread)
        levels = dot(level.astype(F32).astype(BF16), spread)
        wanted = (iota((block, slots), 1) % cap + 1).astype(F32)
        mix_ref[...] = jnp.where(ranks == wanted, levels * (1.0 / 256.0), 0.0).astype(BF16)

    out_ref[...] = (h_ref[...] + dot(mix_ref[...], back_ref[...])).astype(BF16)


def per_device(
    layer_input, queries, keys_in, values_in, decay_rate, attn_gain, norm_gain, expert_ids, gate_levels, w_gate, w_up, w_down
):
    x, q, k, v, decay = layer_input[0], queries[0], keys_in[0], values_in[0], decay_rate[0]
    ids, levels = expert_ids[0], gate_levels[0]
    gate, up, down = w_gate[0], w_up[0], w_down[0]
    block, width = x.shape
    heads = decay.shape[1]
    dh = width // heads
    groups = lax.axis_size("seq")
    experts = lax.axis_size("exp")
    cap = 3 * block // experts
    slots = experts * cap
    hidden = gate.shape[1]
    rows = heads // groups * dh

    states, cum, cum_t = call(
        contrib_body,
        (
            jax.ShapeDtypeStruct((groups, rows + LOG_ROWS, dh), BF16),
            jax.ShapeDtypeStruct((block, heads), F32),
            jax.ShapeDtypeStruct((heads, block), F32),
        ),
        name="contrib",
    )(k, v, decay)
    states = lax.all_to_all(states, "seq", 0, 0, tiled=True)
    carried = call(prefix_body, jax.ShapeDtypeStruct((groups, rows, dh), BF16), name="prefix")(states)
    carried = lax.all_to_all(carried, "seq", 0, 0, tiled=True)
    intra = call(intra_body, jax.ShapeDtypeStruct((block, width), F32), name="intra")(q, k, v, cum, cum_t)
    h_res, send = call(
        finish_body,
        (jax.ShapeDtypeStruct((block, width), F32), jax.ShapeDtypeStruct((slots, width), BF16)),
        scratch_shapes=[pltpu.VMEM((block, width), BF16)],
        name="finish",
    )(intra, q, carried, cum, x, attn_gain[None], norm_gain[None], ids.T)

    got = lax.all_to_all(send.reshape(experts, cap, width), "exp", 0, 0, tiled=True).reshape(slots, width)

    hidden_block = 256
    hidden_steps = hidden // hidden_block
    out_block = 512
    out_steps = width // out_block
    last = hidden_steps - 1
    done = call(
        lambda *refs: expert_body(*refs, hidden_steps=hidden_steps, hidden_block=hidden_block),
        jax.ShapeDtypeStruct((slots, width), BF16),
        grid=(hidden_steps + out_steps,),
        in_specs=[
            pl.BlockSpec((slots, width), lambda i: (0, 0)),
            pl.BlockSpec((width, hidden_block), lambda i: (0, jnp.minimum(i, last))),
            pl.BlockSpec((width, hidden_block), lambda i: (0, jnp.minimum(i, last))),
            pl.BlockSpec((hidden, out_block), lambda i: (0, jnp.maximum(i - hidden_steps, 0))),
        ],
        out_specs=pl.BlockSpec((slots, out_block), lambda i: (0, jnp.maximum(i - hidden_steps, 0))),
        scratch_shapes=[pltpu.VMEM((slots, hidden), BF16)],
        name="expert",
    )(got, gate, up, down)

    back = lax.all_to_all(done.reshape(experts, cap, width), "exp", 0, 0, tiled=True).reshape(slots, width)

    out = call(
        combine_body,
        jax.ShapeDtypeStruct((block, width), BF16),
        grid=(width // out_block,),
        in_specs=[
            pl.BlockSpec((slots, out_block), lambda i: (0, i)),
            pl.BlockSpec((block, out_block), lambda i: (0, i)),
            pl.BlockSpec(ids.shape, lambda i: (0, 0)),
            pl.BlockSpec(levels.shape, lambda i: (0, 0)),
        ],
        out_specs=pl.BlockSpec((block, out_block), lambda i: (0, i)),
        scratch_shapes=[pltpu.VMEM((block, slots), BF16)],
        name="combine",
    )(back, h_res, ids, levels)
    return out[None]


def solution(mesh):
    tokens = P("exp", "seq", None)
    whole = P()
    weights = P("exp", None, None)
    return jax.shard_map(
        per_device,
        mesh=mesh,
        in_specs=(tokens,) * 5 + (whole,) * 2 + (tokens,) * 2 + (weights,) * 3,
        out_specs=tokens,
        check_vma=False,
    )
```

```python
import jax
import jax.numpy as jnp
from jax import lax
from jax.experimental import pallas as pl
from jax.experimental.pallas import tpu as pltpu
from jax.sharding import PartitionSpec as P

F32 = jnp.float32
BF16 = jnp.bfloat16
EXACT = lax.Precision.HIGHEST
VMEM_LIMIT = 24 * 1024 * 1024
PIECES = 3
LOG_ROWS = 32

VMEM_SPEC = pl.BlockSpec(memory_space=pltpu.VMEM)
SMEM_SPEC = pl.BlockSpec(memory_space=pltpu.SMEM)


def near(x):
    return pltpu.with_memory_space_constraint(x, pltpu.VMEM)


def local(body, name, outs, *args, scalars=None, scratch=()):
    specs = [VMEM_SPEC] * len(args)
    given = [near(a) for a in args]
    if scalars is not None:
        specs, given = [SMEM_SPEC, *specs], [scalars, *given]
    made = pl.pallas_call(
        body,
        out_shape=tuple(pltpu.VMEM(shape, dtype) for shape, dtype in outs),
        in_specs=specs,
        out_specs=tuple(VMEM_SPEC for _ in outs),
        scratch_shapes=list(scratch),
        compiler_params=pltpu.CompilerParams(vmem_limit_bytes=VMEM_LIMIT),
        name=name,
    )(*given)
    return made[0] if len(outs) == 1 else made


def dot(a, b, ca=1, cb=0, precision=None):
    return lax.dot_general(
        a, b, (((ca,), (cb,)), ((), ())), precision=precision, preferred_element_type=F32
    )


def iota(shape, dim):
    return lax.broadcasted_iota(jnp.int32, shape, dim)


def log_rows(logs, dh):
    row = iota((LOG_ROWS, dh), 0)
    out = jnp.zeros((LOG_ROWS, dh), F32)
    for i, rest in enumerate(logs):
        for piece in range(PIECES):
            part = rest.astype(BF16).astype(F32)
            out = jnp.where(row == PIECES * i + piece, part, out)
            rest = rest - part
    return out.astype(BF16)


def log_of(ref, i):
    first = ref.shape[0] - LOG_ROWS + PIECES * i
    a, b, c = (ref[first + p : first + p + 1, :].astype(F32) for p in range(PIECES))
    return a + b + c


def contrib_body(half_ref, k_ref, v_ref, decay_ref, out_ref):
    heads, block = decay_ref.shape
    dh = k_ref.shape[1] // heads
    lower = (iota((block, block), 0) >= iota((block, block), 1)).astype(F32)
    cum = -dot(lower, decay_ref[...], 1, 1, precision=EXACT)
    total = cum[block - 1 : block, :]
    decayed = jnp.exp(total - cum)
    logs = []
    for h in range(heads):
        cols = slice(h * dh, (h + 1) * dh)
        kw = (k_ref[:, cols].astype(F32) * decayed[:, h : h + 1]).astype(BF16)
        out_ref[cols, :] = dot(kw, v_ref[:, cols], 0, 0).astype(BF16)
        logs.append(jnp.broadcast_to(total[:, h : h + 1], (1, dh)))
    out_ref[heads * dh :, :] = log_rows(logs, dh)


def pair_body(place_ref, own_ref, other_ref, out_ref):
    dh = own_ref.shape[1]
    heads = (own_ref.shape[0] - LOG_ROWS) // dh
    is_even = place_ref[0] == 0
    logs = []
    for h in range(heads):
        rows = slice(h * dh, (h + 1) * dh)
        own, other = own_ref[rows, :].astype(F32), other_ref[rows, :].astype(F32)
        own_log, other_log = log_of(own_ref, h), log_of(other_ref, h)
        even, odd = jnp.where(is_even, own, other), jnp.where(is_even, other, own)
        out_ref[rows, :] = (jnp.exp(jnp.where(is_even, other_log, own_log)) * even + odd).astype(BF16)
        logs.append(own_log + other_log)
    out_ref[heads * dh :, :] = log_rows(logs, dh)


def carry_body(place_ref, own_ref, other_ref, *refs):
    *earlier, keep_ref, send_ref = refs
    dh = own_ref.shape[1]
    heads = keep_ref.shape[0] // dh
    is_even = place_ref[0] == 0
    chip = place_ref[1]
    for h in range(heads):
        rows = slice(h * dh, (h + 1) * dh)
        state = jnp.zeros((dh, dh), F32)
        for back in range(len(earlier), 0, -1):
            ref = earlier[back - 1]
            joined = jnp.exp(log_of(ref, h)) * state + ref[rows, :].astype(F32)
            state = jnp.where(chip >= back, joined, 0.0)
        even = jnp.where(is_even, own_ref[rows, :].astype(F32), other_ref[rows, :].astype(F32))
        even_log = jnp.where(is_even, log_of(own_ref, h), log_of(other_ref, h))
        after = jnp.exp(even_log) * state + even
        keep_ref[rows, :] = jnp.where(is_even, state, after).astype(BF16)
        send_ref[rows, :] = jnp.where(is_even, after, state).astype(BF16)


def intra_body(q_ref, k_ref, v_ref, decay_ref, out_ref, grow_ref):
    heads, block = decay_ref.shape
    dh = q_ref.shape[1] // heads
    half = block // 2
    lower = (iota((block, block), 0) >= iota((block, block), 1)).astype(F32)
    decay = decay_ref[...]
    cum = -dot(lower, decay, 1, 1, precision=EXACT)
    cum_t = -dot(decay, lower, 1, 1, precision=EXACT)
    grow_ref[...] = jnp.exp(cum)
    for h in range(heads):
        cols = slice(h * dh, (h + 1) * dh)
        for lo, hi in ((0, half), (half, block)):
            scores = dot(q_ref[lo:hi, cols], k_ref[:hi, cols], 1, 1)
            gap = cum[lo:hi, h : h + 1] - cum_t[h : h + 1, :hi]
            seen = iota((hi - lo, hi), 0) + lo >= iota((hi - lo, hi), 1)
            probs = jnp.where(seen, scores * jnp.exp(jnp.minimum(gap, 0.0)), 0.0).astype(BF16)
            out_ref[lo:hi, cols] = dot(probs, v_ref[:hi, cols])


def route_body(ids_ref, levels_ref, pick_ref, mix_ref, *, cap):
    slots, block = pick_ref.shape
    experts = slots // cap
    expert = iota((experts, block), 0)
    first = ids_ref[0:1, :] == expert
    second = ids_ref[1:2, :] == expert
    member = (first | second).astype(F32)
    earlier = (iota((block, block), 0) < iota((block, block), 1)).astype(BF16)
    rank = ((dot(member.astype(BF16), earlier) + 1.0) * member).astype(BF16)
    level = jnp.where(first, levels_ref[0:1, :], 0) + jnp.where(second, levels_ref[1:2, :], 0)
    level = level.astype(F32).astype(BF16)
    spread = (iota((slots, experts), 0) // cap == iota((slots, experts), 1)).astype(BF16)
    pick_ref[...] = (dot(spread, rank) == (iota((slots, block), 0) % cap + 1).astype(F32)).astype(BF16)
    spread = (iota((experts, slots), 1) // cap == iota((experts, slots), 0)).astype(BF16)
    used = dot(rank, spread, 0, 0) == (iota((block, slots), 1) % cap + 1).astype(F32)
    mix_ref[...] = jnp.where(used, dot(level, spread, 0, 0) * (1.0 / 256.0), 0.0).astype(BF16)


def finish_body(
    place_ref, intra_ref, q_ref, keep_ref, got_ref, grow_ref, x_ref, attn_gain_ref, norm_gain_ref, pick_ref, h_ref, send_ref
):
    block, heads = grow_ref.shape
    width = q_ref.shape[1]
    dh = width // heads
    per = heads // 2
    core = place_ref[0]
    squares = jnp.zeros((block, dh), F32)
    for h in range(heads):
        cols = slice(h * dh, (h + 1) * dh)
        rows = slice(h % per * dh, (h % per + 1) * dh)
        state = jnp.where(core == h // per, keep_ref[rows, :].astype(F32), got_ref[rows, :].astype(F32))
        raw = intra_ref[:, cols] + grow_ref[:, h : h + 1] * dot(q_ref[:, cols], state.astype(BF16))
        scale = lax.rsqrt(jnp.mean(raw * raw, axis=-1, keepdims=True) + 1e-06)
        res = x_ref[:, cols].astype(F32) + attn_gain_ref[:, cols] * (raw * scale)
        h_ref[:, cols] = res
        squares = squares + res * res
    scale = lax.rsqrt(jnp.sum(squares, axis=-1, keepdims=True) / width + 1e-06)
    step = 512
    for c in range(0, width, step):
        cols = slice(c, c + step)
        normed = (norm_gain_ref[:, cols] * h_ref[:, cols] * scale).astype(BF16)
        send_ref[:, cols] = dot(pick_ref[...], normed).astype(BF16)


def expert_body(x_ref, gate_ref, up_ref, down_ref, out_ref, act_ref):
    hidden, width = down_ref.shape
    step = 256
    for c in range(0, hidden, step):
        cols = slice(c, c + step)
        gate = dot(x_ref[...], gate_ref[:, cols])
        up = dot(x_ref[...], up_ref[:, cols])
        act_ref[:, cols] = (gate / (1.0 + jnp.exp(-gate)) * up).astype(BF16)
    for c in range(0, width, step):
        cols = slice(c, c + step)
        out_ref[:, cols] = dot(act_ref[...], down_ref[:, cols]).astype(BF16)


def combine_body(back_ref, h_ref, mix_ref, out_ref):
    step = 512
    for c in range(0, h_ref.shape[1], step):
        cols = slice(c, c + step)
        out_ref[:, cols] = (h_ref[:, cols] + dot(mix_ref[...], back_ref[:, cols])).astype(BF16)


def contribution(half, k, v, decay_t):
    heads, block = decay_t.shape
    width = k.shape[1]
    dh = width // heads
    return pl.pallas_call(
        contrib_body,
        out_shape=pltpu.VMEM((width // 2 + LOG_ROWS, dh), BF16),
        grid_spec=pltpu.PrefetchScalarGridSpec(
            num_scalar_prefetch=1,
            grid=(1,),
            in_specs=[
                pl.BlockSpec((block, width // 2), lambda i, half: (0, half[0])),
                pl.BlockSpec((block, width // 2), lambda i, half: (0, half[0])),
                pl.BlockSpec((heads // 2, block), lambda i, half: (half[0], 0)),
            ],
            out_specs=VMEM_SPEC,
        ),
        compiler_params=pltpu.CompilerParams(vmem_limit_bytes=VMEM_LIMIT),
        name="contrib",
    )(half, k, v, decay_t)


def carried_states(k, v, decay_t, place):
    blocks = lax.axis_size("seq")
    chips = blocks // 2
    dh = k.shape[1] // decay_t.shape[0]
    core = place[:1]
    swap = [(i, i ^ 1) for i in range(blocks)]

    def along(by):
        return [(i, (i // 2 + by) % chips * 2 + i % 2) for i in range(blocks)]

    other = lax.ppermute(contribution(1 - core, k, v, decay_t), "seq", swap)
    own = contribution(core, k, v, decay_t)
    pair = local(pair_body, "pair", [(own.shape, BF16)], own, other, scalars=place)
    earlier = [lax.ppermute(pair, "seq", along(by)) for by in range(1, chips)]
    half = ((own.shape[0] - LOG_ROWS, dh), BF16)
    keep, send = local(carry_body, "carry", [half, half], own, other, *earlier, scalars=place)
    return keep, lax.ppermute(send, "seq", swap)


def per_device(
    layer_input, queries, keys_in, values_in, decay_rate, attn_gain, norm_gain, expert_ids, gate_levels, w_gate, w_up, w_down
):
    x, q, k, v, decay_t = layer_input[0], queries[0], keys_in[0], values_in[0], decay_rate[0].T
    block, width = x.shape
    heads = decay_t.shape[0]
    experts = lax.axis_size("exp")
    cap = 3 * block // experts
    slots = experts * cap
    hidden = w_gate.shape[2]
    index = lax.axis_index("seq")
    place = jnp.stack([index % 2, index // 2]).astype(jnp.int32)

    keep, got = carried_states(k, v, decay_t, place)
    intra, grow = local(
        intra_body, "intra", [((block, width), F32), ((block, heads), F32)], q, k, v, decay_t
    )
    pick, mix = local(
        lambda *refs: route_body(*refs, cap=cap),
        "route",
        [((slots, block), BF16), ((block, slots), BF16)],
        expert_ids[0].T,
        gate_levels[0].T,
    )
    h_res, send = local(
        finish_body,
        "finish",
        [((block, width), F32), ((slots, width), BF16)],
        *(intra, q, keep, got, grow, x, attn_gain[None], norm_gain[None], pick),
        scalars=place,
    )
    arrived = lax.all_to_all(send.reshape(experts, cap, width), "exp", 0, 0, tiled=True)
    done = local(
        expert_body,
        "expert",
        [((slots, width), BF16)],
        *(arrived.reshape(slots, width), w_gate[0], w_up[0], w_down[0]),
        scratch=[pltpu.VMEM((slots, hidden), BF16)],
    )
    back = lax.all_to_all(done.reshape(experts, cap, width), "exp", 0, 0, tiled=True)
    out = local(
        combine_body, "combine", [((block, width), BF16)], back.reshape(slots, width), h_res, mix
    )
    return out[None]


def solution(mesh):
    tokens = P("exp", "seq", None)
    whole = P()
    weights = P("exp", None, None)
    return jax.shard_map(
        per_device,
        mesh=mesh,
        in_specs=(tokens,) * 5 + (whole,) * 2 + (tokens,) * 2 + (weights,) * 3,
        out_specs=tokens,
        check_vma=False,
    )
```

```python
import jax
import jax.numpy as jnp
from jax import lax
from jax.experimental import pallas as pl
from jax.experimental.pallas import tpu as pltpu
from jax.sharding import PartitionSpec as P

F32 = jnp.float32
BF16 = jnp.bfloat16
EXACT = lax.Precision.HIGHEST
VMEM_LIMIT = 24 * 1024 * 1024
PIECES = 3
LOG_ROWS = 32

VMEM_SPEC = pl.BlockSpec(memory_space=pltpu.VMEM)
SMEM_SPEC = pl.BlockSpec(memory_space=pltpu.SMEM)


def near(x):
    return pltpu.with_memory_space_constraint(x, pltpu.VMEM)


def local(body, name, outs, *args, scalars=None, scratch=()):
    specs = [VMEM_SPEC] * len(args)
    given = [near(a) for a in args]
    if scalars is not None:
        specs, given = [SMEM_SPEC, *specs], [scalars, *given]
    made = pl.pallas_call(
        body,
        out_shape=tuple(pltpu.VMEM(shape, dtype) for shape, dtype in outs),
        in_specs=specs,
        out_specs=tuple(VMEM_SPEC for _ in outs),
        scratch_shapes=list(scratch),
        compiler_params=pltpu.CompilerParams(vmem_limit_bytes=VMEM_LIMIT),
        name=name,
    )(*given)
    return made[0] if len(outs) == 1 else made


def dot(a, b, ca=1, cb=0, precision=None):
    return lax.dot_general(
        a, b, (((ca,), (cb,)), ((), ())), precision=precision, preferred_element_type=F32
    )


def iota(shape, dim):
    return lax.broadcasted_iota(jnp.int32, shape, dim)


def log_rows(logs, dh):
    row = iota((LOG_ROWS, dh), 0)
    out = jnp.zeros((LOG_ROWS, dh), F32)
    for i, rest in enumerate(logs):
        for piece in range(PIECES):
            part = rest.astype(BF16).astype(F32)
            out = jnp.where(row == PIECES * i + piece, part, out)
            rest = rest - part
    return out.astype(BF16)


def log_of(ref, i):
    first = ref.shape[0] - LOG_ROWS + PIECES * i
    a, b, c = (ref[first + p : first + p + 1, :].astype(F32) for p in range(PIECES))
    return a + b + c


def contrib_body(half_ref, k_ref, v_ref, decay_ref, out_ref):
    heads, block = decay_ref.shape
    dh = k_ref.shape[1] // heads
    lower = (iota((block, block), 0) >= iota((block, block), 1)).astype(F32)
    cum = -dot(lower, decay_ref[...], 1, 1, precision=EXACT)
    total = cum[block - 1 : block, :]
    decayed = jnp.exp(total - cum)
    logs = []
    for h in range(heads):
        cols = slice(h * dh, (h + 1) * dh)
        kw = (k_ref[:, cols].astype(F32) * decayed[:, h : h + 1]).astype(BF16)
        out_ref[cols, :] = dot(kw, v_ref[:, cols], 0, 0).astype(BF16)
        logs.append(jnp.broadcast_to(total[:, h : h + 1], (1, dh)))
    out_ref[heads * dh :, :] = log_rows(logs, dh)


def pair_body(place_ref, own_ref, other_ref, out_ref):
    dh = own_ref.shape[1]
    heads = (own_ref.shape[0] - LOG_ROWS) // dh
    is_even = place_ref[0] == 0
    logs = []
    for h in range(heads):
        rows = slice(h * dh, (h + 1) * dh)
        own, other = own_ref[rows, :].astype(F32), other_ref[rows, :].astype(F32)
        own_log, other_log = log_of(own_ref, h), log_of(other_ref, h)
        even, odd = jnp.where(is_even, own, other), jnp.where(is_even, other, own)
        out_ref[rows, :] = (jnp.exp(jnp.where(is_even, other_log, own_log)) * even + odd).astype(BF16)
        logs.append(own_log + other_log)
    out_ref[heads * dh :, :] = log_rows(logs, dh)


def carry_body(place_ref, own_ref, other_ref, *refs):
    *earlier, keep_ref, send_ref = refs
    dh = own_ref.shape[1]
    heads = keep_ref.shape[0] // dh
    is_even = place_ref[0] == 0
    chip = place_ref[1]
    for h in range(heads):
        rows = slice(h * dh, (h + 1) * dh)
        state = jnp.zeros((dh, dh), F32)
        for back in range(len(earlier), 0, -1):
            ref = earlier[back - 1]
            joined = jnp.exp(log_of(ref, h)) * state + ref[rows, :].astype(F32)
            state = jnp.where(chip >= back, joined, 0.0)
        even = jnp.where(is_even, own_ref[rows, :].astype(F32), other_ref[rows, :].astype(F32))
        even_log = jnp.where(is_even, log_of(own_ref, h), log_of(other_ref, h))
        after = jnp.exp(even_log) * state + even
        keep_ref[rows, :] = jnp.where(is_even, state, after).astype(BF16)
        send_ref[rows, :] = jnp.where(is_even, after, state).astype(BF16)


def intra_body(q_ref, k_ref, v_ref, decay_ref, out_ref, grow_ref):
    heads, block = decay_ref.shape
    dh = q_ref.shape[1] // heads
    half = block // 2
    lower = (iota((block, block), 0) >= iota((block, block), 1)).astype(F32)
    decay = decay_ref[...]
    cum = -dot(lower, decay, 1, 1, precision=EXACT)
    cum_t = -dot(decay, lower, 1, 1, precision=EXACT)
    grow_ref[...] = jnp.exp(cum)
    for h in range(heads):
        cols = slice(h * dh, (h + 1) * dh)
        for lo, hi in ((0, half), (half, block)):
            scores = dot(q_ref[lo:hi, cols], k_ref[:hi, cols], 1, 1)
            gap = cum[lo:hi, h : h + 1] - cum_t[h : h + 1, :hi]
            seen = iota((hi - lo, hi), 0) + lo >= iota((hi - lo, hi), 1)
            probs = jnp.where(seen, scores * jnp.exp(jnp.minimum(gap, 0.0)), 0.0).astype(BF16)
            out_ref[lo:hi, cols] = dot(probs, v_ref[:hi, cols])


def route_body(ids_ref, levels_ref, pick_ref, mix_ref, *, cap):
    slots, block = pick_ref.shape
    experts = slots // cap
    expert = iota((experts, block), 0)
    first = ids_ref[0:1, :] == expert
    second = ids_ref[1:2, :] == expert
    member = (first | second).astype(F32)
    earlier = (iota((block, block), 0) < iota((block, block), 1)).astype(BF16)
    rank = ((dot(member.astype(BF16), earlier) + 1.0) * member).astype(BF16)
    level = jnp.where(first, levels_ref[0:1, :], 0) + jnp.where(second, levels_ref[1:2, :], 0)
    level = level.astype(F32).astype(BF16)
    spread = (iota((slots, experts), 0) // cap == iota((slots, experts), 1)).astype(BF16)
    pick_ref[...] = (dot(spread, rank) == (iota((slots, block), 0) % cap + 1).astype(F32)).astype(BF16)
    spread = (iota((experts, slots), 1) // cap == iota((experts, slots), 0)).astype(BF16)
    used = dot(rank, spread, 0, 0) == (iota((block, slots), 1) % cap + 1).astype(F32)
    mix_ref[...] = jnp.where(used, dot(level, spread, 0, 0) * (1.0 / 256.0), 0.0).astype(BF16)


def finish_body(
    place_ref, intra_ref, q_ref, keep_ref, got_ref, grow_ref, x_ref, attn_gain_ref, norm_gain_ref, pick_ref, h_ref, send_ref
):
    block, heads = grow_ref.shape
    width = q_ref.shape[1]
    dh = width // heads
    per = heads // 2
    core = place_ref[0]
    squares = jnp.zeros((block, dh), F32)
    for h in range(heads):
        cols = slice(h * dh, (h + 1) * dh)
        rows = slice(h % per * dh, (h % per + 1) * dh)
        state = jnp.where(core == h // per, keep_ref[rows, :].astype(F32), got_ref[rows, :].astype(F32))
        raw = intra_ref[:, cols] + grow_ref[:, h : h + 1] * dot(q_ref[:, cols], state.astype(BF16))
        scale = lax.rsqrt(jnp.mean(raw * raw, axis=-1, keepdims=True) + 1e-06)
        res = x_ref[:, cols].astype(F32) + attn_gain_ref[:, cols] * (raw * scale)
        h_ref[:, cols] = res
        squares = squares + res * res
    scale = lax.rsqrt(jnp.sum(squares, axis=-1, keepdims=True) / width + 1e-06)
    step = 512
    for c in range(0, width, step):
        cols = slice(c, c + step)
        normed = (norm_gain_ref[:, cols] * h_ref[:, cols] * scale).astype(BF16)
        send_ref[:, cols] = dot(pick_ref[...], normed).astype(BF16)


def expert_body(x_ref, gate_ref, up_ref, down_ref, out_ref, act_ref):
    hidden, width = down_ref.shape
    step = 256
    for c in range(0, hidden, step):
        cols = slice(c, c + step)
        gate = dot(x_ref[...], gate_ref[:, cols])
        up = dot(x_ref[...], up_ref[:, cols])
        act_ref[:, cols] = (gate / (1.0 + jnp.exp(-gate)) * up).astype(BF16)
    for c in range(0, width, step):
        cols = slice(c, c + step)
        out_ref[:, cols] = dot(act_ref[...], down_ref[:, cols]).astype(BF16)


def combine_body(back_ref, h_ref, mix_ref, out_ref):
    step = out_ref.shape[1]
    cols = pl.ds(pl.multiple_of(pl.program_id(0) * step, 128), step)
    out_ref[...] = (h_ref[:, cols] + dot(mix_ref[...], back_ref[:, cols])).astype(BF16)


def combine(back, h_res, mix):
    block, width = h_res.shape
    step = 512
    return pl.pallas_call(
        combine_body,
        out_shape=jax.ShapeDtypeStruct((block, width), BF16),
        grid=(width // step,),
        in_specs=[VMEM_SPEC] * 3,
        out_specs=pl.BlockSpec((block, step), lambda i: (0, i)),
        compiler_params=pltpu.CompilerParams(vmem_limit_bytes=VMEM_LIMIT),
        name="combine",
    )(near(back), near(h_res), near(mix))


def contribution(half, k, v, decay_t):
    heads, block = decay_t.shape
    width = k.shape[1]
    dh = width // heads
    return pl.pallas_call(
        contrib_body,
        out_shape=pltpu.VMEM((width // 2 + LOG_ROWS, dh), BF16),
        grid_spec=pltpu.PrefetchScalarGridSpec(
            num_scalar_prefetch=1,
            grid=(1,),
            in_specs=[
                pl.BlockSpec((block, width // 2), lambda i, half: (0, half[0])),
                pl.BlockSpec((block, width // 2), lambda i, half: (0, half[0])),
                pl.BlockSpec((heads // 2, block), lambda i, half: (half[0], 0)),
            ],
            out_specs=VMEM_SPEC,
        ),
        compiler_params=pltpu.CompilerParams(vmem_limit_bytes=VMEM_LIMIT),
        name="contrib",
    )(half, *(pltpu.with_memory_space_constraint(a, pltpu.HBM) for a in (k, v, decay_t)))


def pair_states(k, v, decay_t, place):
    swap = [(i, i ^ 1) for i in range(lax.axis_size("seq"))]
    core = place[:1]
    other = lax.ppermute(contribution(1 - core, k, v, decay_t), "seq", swap)
    own = contribution(core, k, v, decay_t)
    return own, other, local(pair_body, "pair", [(own.shape, BF16)], own, other, scalars=place)


def of_earlier_chips(pair):
    blocks = lax.axis_size("seq")
    chips = blocks // 2
    return [
        lax.ppermute(pair, "seq", [(i, (i // 2 + by) % chips * 2 + i % 2) for i in range(blocks)])
        for by in range(1, chips)
    ]


def carried_states(own, other, earlier, place):
    swap = [(i, i ^ 1) for i in range(lax.axis_size("seq"))]
    half = ((own.shape[0] - LOG_ROWS, own.shape[1]), BF16)
    keep, send = local(carry_body, "carry", [half, half], own, other, *earlier, scalars=place)
    return keep, lax.ppermute(send, "seq", swap)


def per_device(
    layer_input, queries, keys_in, values_in, decay_rate, attn_gain, norm_gain, expert_ids, gate_levels, w_gate, w_up, w_down
):
    x, q, k, v, decay_t = layer_input[0], queries[0], keys_in[0], values_in[0], decay_rate[0].T
    block, width = x.shape
    heads = decay_t.shape[0]
    experts = lax.axis_size("exp")
    cap = 3 * block // experts
    slots = experts * cap
    hidden = w_gate.shape[2]
    index = lax.axis_index("seq")
    place = jnp.stack([index % 2, index // 2]).astype(jnp.int32)

    own, other, pair = pair_states(k, v, decay_t, place)
    pair, q, ids = lax.optimization_barrier((pair, q, expert_ids[0]))
    earlier = of_earlier_chips(pair)
    intra, grow = local(
        intra_body, "intra", [((block, width), F32), ((block, heads), F32)], q, k, v, decay_t
    )
    pick, mix = local(
        lambda *refs: route_body(*refs, cap=cap),
        "route",
        [((slots, block), BF16), ((block, slots), BF16)],
        ids.T,
        gate_levels[0].T,
    )
    earlier, intra, grow, pick, mix = lax.optimization_barrier((earlier, intra, grow, pick, mix))
    keep, got = carried_states(own, other, earlier, place)
    h_res, send = local(
        finish_body,
        "finish",
        [((block, width), F32), ((slots, width), BF16)],
        *(intra, q, keep, got, grow, x, attn_gain[None], norm_gain[None], pick),
        scalars=place,
    )
    arrived = lax.all_to_all(send.reshape(experts, cap, width), "exp", 0, 0, tiled=True)
    done = local(
        expert_body,
        "expert",
        [((slots, width), BF16)],
        *(arrived.reshape(slots, width), w_gate[0], w_up[0], w_down[0]),
        scratch=[pltpu.VMEM((slots, hidden), BF16)],
    )
    back = lax.all_to_all(done.reshape(experts, cap, width), "exp", 0, 0, tiled=True)
    return combine(back.reshape(slots, width), h_res, mix)[None]


def solution(mesh):
    tokens = P("exp", "seq", None)
    whole = P()
    weights = P("exp", None, None)
    return jax.shard_map(
        per_device,
        mesh=mesh,
        in_specs=(tokens,) * 5 + (whole,) * 2 + (tokens,) * 2 + (weights,) * 3,
        out_specs=tokens,
        check_vma=False,
    )
```

```python
import jax
import jax.numpy as jnp
from jax import lax
from jax.experimental import pallas as pl
from jax.experimental.pallas import tpu as pltpu
from jax.sharding import PartitionSpec as P

F32 = jnp.float32
BF16 = jnp.bfloat16
EXACT = lax.Precision.HIGHEST
VMEM_LIMIT = 24 * 1024 * 1024
PIECES = 3
LOG_ROWS = 32

VMEM_SPEC = pl.BlockSpec(memory_space=pltpu.VMEM)
SMEM_SPEC = pl.BlockSpec(memory_space=pltpu.SMEM)


def near(x):
    return pltpu.with_memory_space_constraint(x, pltpu.VMEM)


def far(x):
    return pltpu.with_memory_space_constraint(x, pltpu.HBM)


def local(body, name, outs, *args, scalars=(), scratch=()):
    made = pl.pallas_call(
        body,
        out_shape=tuple(pltpu.VMEM(shape, dtype) for shape, dtype in outs),
        grid_spec=pltpu.PrefetchScalarGridSpec(
            num_scalar_prefetch=len(scalars),
            grid=(1,),
            in_specs=[VMEM_SPEC] * len(args),
            out_specs=tuple(VMEM_SPEC for _ in outs),
            scratch_shapes=list(scratch),
        ),
        compiler_params=pltpu.CompilerParams(vmem_limit_bytes=VMEM_LIMIT),
        name=name,
    )(*scalars, *(near(a) for a in args))
    return made[0] if len(outs) == 1 else made


def dot(a, b, ca=1, cb=0, precision=None):
    return lax.dot_general(
        a, b, (((ca,), (cb,)), ((), ())), precision=precision, preferred_element_type=F32
    )


def iota(shape, dim):
    return lax.broadcasted_iota(jnp.int32, shape, dim)


def log_rows(logs, dh):
    row = iota((LOG_ROWS, dh), 0)
    out = jnp.zeros((LOG_ROWS, dh), F32)
    for i, rest in enumerate(logs):
        for piece in range(PIECES):
            part = rest.astype(BF16).astype(F32)
            out = jnp.where(row == PIECES * i + piece, part, out)
            rest = rest - part
    return out.astype(BF16)


def log_of(ref, i):
    first = ref.shape[0] - LOG_ROWS + PIECES * i
    a, b, c = (ref[first + p : first + p + 1, :].astype(F32) for p in range(PIECES))
    return a + b + c


def contrib_body(half_ref, k_ref, v_ref, decay_ref, out_ref, decayed_ref):
    heads, block = decay_ref.shape
    steps = pl.num_programs(0)
    dh = out_ref.shape[1]
    per = k_ref.shape[1] // dh
    step = pl.program_id(0)

    @pl.when(step == 0)
    def _():
        lower = (iota((block, block), 0) >= iota((block, block), 1)).astype(F32)
        cum = -dot(lower, decay_ref[...], 1, 1, precision=EXACT)
        total = cum[block - 1 : block, :]
        decayed_ref[...] = jnp.exp(total - cum)
        logs = [jnp.broadcast_to(total[:, h : h + 1], (1, dh)) for h in range(heads)]
        out_ref[heads * dh :, :] = log_rows(logs, dh)

    for i in range(per):
        cols = slice(i * dh, (i + 1) * dh)
        weight = decayed_ref[:, i : i + 1]
        for later in range(per, heads, per):
            weight = jnp.where(step == later // per, decayed_ref[:, later + i : later + i + 1], weight)
        kw = (k_ref[:, cols].astype(F32) * weight).astype(BF16)
        rows = pl.ds(pl.multiple_of((step * per + i) * dh, dh), dh)
        out_ref[rows, :] = dot(kw, v_ref[:, cols], 0, 0).astype(BF16)


def pair_body(core_ref, own_ref, other_ref, out_ref):
    dh = own_ref.shape[1]
    heads = (own_ref.shape[0] - LOG_ROWS) // dh
    is_even = core_ref[0] == 0
    logs = []
    for h in range(heads):
        rows = slice(h * dh, (h + 1) * dh)
        own, other = own_ref[rows, :].astype(F32), other_ref[rows, :].astype(F32)
        own_log, other_log = log_of(own_ref, h), log_of(other_ref, h)
        even, odd = jnp.where(is_even, own, other), jnp.where(is_even, other, own)
        out_ref[rows, :] = (jnp.exp(jnp.where(is_even, other_log, own_log)) * even + odd).astype(BF16)
        logs.append(own_log + other_log)
    out_ref[heads * dh :, :] = log_rows(logs, dh)


def carry_body(core_ref, chip_ref, own_ref, other_ref, *refs):
    *earlier, keep_ref, send_ref = refs
    dh = own_ref.shape[1]
    heads = keep_ref.shape[0] // dh
    is_even = core_ref[0] == 0
    chip = chip_ref[0]
    for h in range(heads):
        rows = slice(h * dh, (h + 1) * dh)
        state = jnp.zeros((dh, dh), F32)
        for back in range(len(earlier), 0, -1):
            ref = earlier[back - 1]
            joined = jnp.exp(log_of(ref, h)) * state + ref[rows, :].astype(F32)
            state = jnp.where(chip >= back, joined, 0.0)
        even = jnp.where(is_even, own_ref[rows, :].astype(F32), other_ref[rows, :].astype(F32))
        even_log = jnp.where(is_even, log_of(own_ref, h), log_of(other_ref, h))
        after = jnp.exp(even_log) * state + even
        keep_ref[rows, :] = jnp.where(is_even, state, after).astype(BF16)
        send_ref[rows, :] = jnp.where(is_even, after, state).astype(BF16)


def intra_body(q_ref, k_ref, v_ref, decay_ref, out_ref, grow_ref):
    heads, block = decay_ref.shape
    dh = q_ref.shape[1] // heads
    half = block // 2
    lower = (iota((block, block), 0) >= iota((block, block), 1)).astype(F32)
    decay = decay_ref[...]
    cum = -dot(lower, decay, 1, 1, precision=EXACT)
    cum_t = -dot(decay, lower, 1, 1, precision=EXACT)
    part = pl.program_id(0)
    grow_ref[part] = jnp.exp(cum)
    for h in range(heads):
        cols = slice(h * dh, (h + 1) * dh)
        for lo, hi in ((0, half), (half, block)):
            scores = dot(q_ref[lo:hi, cols], k_ref[:hi, cols], 1, 1)
            gap = cum[lo:hi, h : h + 1] - cum_t[h : h + 1, :hi]
            seen = iota((hi - lo, hi), 0) + lo >= iota((hi - lo, hi), 1)
            probs = jnp.where(seen, scores * jnp.exp(jnp.minimum(gap, 0.0)), 0.0).astype(BF16)
            out_ref[part, lo:hi, cols] = dot(probs, v_ref[:hi, cols])


def route_body(ids_ref, levels_ref, pick_ref, mix_ref, *, cap):
    slots, block = pick_ref.shape
    experts = slots // cap
    expert = iota((experts, block), 0)
    first = ids_ref[0:1, :] == expert
    second = ids_ref[1:2, :] == expert
    member = (first | second).astype(F32)
    earlier = (iota((block, block), 0) < iota((block, block), 1)).astype(BF16)
    rank = ((dot(member.astype(BF16), earlier) + 1.0) * member).astype(BF16)
    level = jnp.where(first, levels_ref[0:1, :], 0) + jnp.where(second, levels_ref[1:2, :], 0)
    level = level.astype(F32).astype(BF16)
    spread = (iota((slots, experts), 0) // cap == iota((slots, experts), 1)).astype(BF16)
    pick_ref[...] = (dot(spread, rank) == (iota((slots, block), 0) % cap + 1).astype(F32)).astype(BF16)
    spread = (iota((experts, slots), 1) // cap == iota((experts, slots), 0)).astype(BF16)
    used = dot(rank, spread, 0, 0) == (iota((block, slots), 1) % cap + 1).astype(F32)
    mix_ref[...] = jnp.where(used, dot(level, spread, 0, 0) * (1.0 / 256.0), 0.0).astype(BF16)


def finish_body(
    core_ref, intra_ref, q_ref, keep_ref, got_ref, grow_ref, x_ref, attn_gain_ref, norm_gain_ref, pick_ref, h_ref, send_ref
):
    block, width = q_ref.shape
    per = grow_ref.shape[2]
    heads = 2 * per
    dh = width // heads
    core = core_ref[0]
    squares = jnp.zeros((block, dh), F32)
    for h in range(heads):
        cols = slice(h * dh, (h + 1) * dh)
        rows = slice(h % per * dh, (h % per + 1) * dh)
        state = jnp.where(core == h // per, keep_ref[rows, :].astype(F32), got_ref[rows, :].astype(F32))
        raw = intra_ref[h // per, :, rows] + grow_ref[h // per, :, h % per : h % per + 1] * dot(q_ref[:, cols], state.astype(BF16))
        scale = lax.rsqrt(jnp.mean(raw * raw, axis=-1, keepdims=True) + 1e-06)
        res = x_ref[:, cols].astype(F32) + attn_gain_ref[:, cols] * (raw * scale)
        h_ref[:, cols] = res
        squares = squares + res * res
    scale = lax.rsqrt(jnp.sum(squares, axis=-1, keepdims=True) / width + 1e-06)
    step = 512
    for c in range(0, width, step):
        cols = slice(c, c + step)
        normed = (norm_gain_ref[:, cols] * h_ref[:, cols] * scale).astype(BF16)
        send_ref[:, cols] = dot(pick_ref[...], normed).astype(BF16)


def expert_body(x_ref, gate_ref, up_ref, down_ref, out_ref, act_ref):
    hidden, width = down_ref.shape
    step = 256
    for c in range(0, hidden, step):
        cols = slice(c, c + step)
        gate = dot(x_ref[...], gate_ref[:, cols])
        up = dot(x_ref[...], up_ref[:, cols])
        act_ref[:, cols] = (gate / (1.0 + jnp.exp(-gate)) * up).astype(BF16)
    for c in range(0, width, step):
        cols = slice(c, c + step)
        out_ref[:, cols] = dot(act_ref[...], down_ref[:, cols]).astype(BF16)


def combine_body(back_ref, h_ref, mix_ref, out_ref, buf, sems):
    parts, _, step = buf.shape
    stores = []
    for i in range(parts):
        cols = slice(i * step, (i + 1) * step)
        buf[i] = (h_ref[:, cols] + dot(mix_ref[...], back_ref[:, cols])).astype(BF16)
        stores.append(pltpu.make_async_copy(buf.at[i], out_ref.at[:, cols], sems.at[i]))
        stores[i].start()
    for store in stores:
        store.wait()


def combine(back, h_res, mix):
    block, width = h_res.shape
    parts = 4
    return pl.pallas_call(
        combine_body,
        out_shape=jax.ShapeDtypeStruct((block, width), BF16),
        in_specs=[VMEM_SPEC] * 3,
        out_specs=pl.BlockSpec(memory_space=pltpu.HBM),
        scratch_shapes=[pltpu.VMEM((parts, block, width // parts), BF16), pltpu.SemaphoreType.DMA((parts,))],
        compiler_params=pltpu.CompilerParams(vmem_limit_bytes=VMEM_LIMIT),
        name="combine",
    )(near(back), near(h_res), near(mix))


def contribution(half, k, v, decay_t, steps=1):
    heads, block = decay_t.shape
    width = k.shape[1]
    dh = width // heads
    columns = pl.BlockSpec((block, width // 2 // steps), lambda i, half: (0, half[0] * steps + i))
    return pl.pallas_call(
        contrib_body,
        out_shape=pltpu.VMEM((width // 2 + LOG_ROWS, dh), BF16),
        grid_spec=pltpu.PrefetchScalarGridSpec(
            num_scalar_prefetch=1,
            grid=(steps,),
            in_specs=[columns, columns, pl.BlockSpec((heads // 2, block), lambda i, half: (half[0], 0))],
            out_specs=VMEM_SPEC,
            scratch_shapes=[pltpu.VMEM((block, heads // 2), F32)],
        ),
        compiler_params=pltpu.CompilerParams(vmem_limit_bytes=VMEM_LIMIT),
        name="contrib",
    )(half, far(k), far(v), far(decay_t))


def inside_block(q, k, v, decay_t):
    heads, block = decay_t.shape
    width = q.shape[1]
    columns = pl.BlockSpec((block, width // 2), lambda i: (0, i))
    return pl.pallas_call(
        intra_body,
        out_shape=(pltpu.VMEM((2, block, width // 2), F32), pltpu.VMEM((2, block, heads // 2), F32)),
        grid=(2,),
        in_specs=[columns, columns, columns, pl.BlockSpec((heads // 2, block), lambda i: (i, 0))],
        out_specs=(VMEM_SPEC, VMEM_SPEC),
        compiler_params=pltpu.CompilerParams(vmem_limit_bytes=VMEM_LIMIT),
        name="intra",
    )(far(q), far(k), far(v), far(decay_t))


def pair_states(k, v, decay_t, core):
    swap = [(i, i ^ 1) for i in range(lax.axis_size("seq"))]
    other = lax.ppermute(contribution(1 - core, k, v, decay_t), "seq", swap)
    own = contribution(core, k, v, decay_t)
    return own, other, local(pair_body, "pair", [(own.shape, BF16)], own, other, scalars=(core,))


def of_earlier_chips(pair):
    blocks = lax.axis_size("seq")
    chips = blocks // 2
    return [
        lax.ppermute(pair, "seq", [(i, (i // 2 + by) % chips * 2 + i % 2) for i in range(blocks)])
        for by in range(1, chips)
    ]


def carried_states(own, other, earlier, core, chip):
    swap = [(i, i ^ 1) for i in range(lax.axis_size("seq"))]
    half = ((own.shape[0] - LOG_ROWS, own.shape[1]), BF16)
    keep, send = local(carry_body, "carry", [half, half], own, other, *earlier, scalars=(core, chip))
    return keep, lax.ppermute(send, "seq", swap)


def per_device(
    layer_input, queries, keys_in, values_in, decay_rate, attn_gain, norm_gain, expert_ids, gate_levels, w_gate, w_up, w_down
):
    x, q, k, v, decay_t = layer_input[0], queries[0], keys_in[0], values_in[0], decay_rate[0].T
    block, width = x.shape
    heads = decay_t.shape[0]
    experts = lax.axis_size("exp")
    cap = 3 * block // experts
    slots = experts * cap
    hidden = w_gate.shape[2]
    index = lax.axis_index("seq").reshape(1)
    core, chip = index & 1, index >> 1

    own, other, pair = pair_states(k, v, decay_t, core)
    pair, q, ids = lax.optimization_barrier((pair, q, expert_ids[0]))
    earlier = of_earlier_chips(pair)
    intra, grow = inside_block(q, k, v, decay_t)
    pick, mix = local(
        lambda *refs: route_body(*refs, cap=cap),
        "route",
        [((slots, block), BF16), ((block, slots), BF16)],
        ids.T,
        gate_levels[0].T,
    )
    earlier, intra, grow, pick, mix = lax.optimization_barrier((earlier, intra, grow, pick, mix))
    keep, got = carried_states(own, other, earlier, core, chip)
    h_res, send = local(
        finish_body,
        "finish",
        [((block, width), F32), ((slots, width), BF16)],
        *(intra, q, keep, got, grow, x, attn_gain[None], norm_gain[None], pick),
        scalars=(core,),
    )
    arrived = lax.all_to_all(send.reshape(experts, cap, width), "exp", 0, 0, tiled=True)
    done = local(
        expert_body,
        "expert",
        [((slots, width), BF16)],
        *(arrived.reshape(slots, width), w_gate[0], w_up[0], w_down[0]),
        scratch=[pltpu.VMEM((slots, hidden), BF16)],
    )
    back = lax.all_to_all(done.reshape(experts, cap, width), "exp", 0, 0, tiled=True)
    return combine(back.reshape(slots, width), h_res, mix)[None]


def solution(mesh):
    tokens = P("exp", "seq", None)
    whole = P()
    weights = P("exp", None, None)
    return jax.shard_map(
        per_device,
        mesh=mesh,
        in_specs=(tokens,) * 5 + (whole,) * 2 + (tokens,) * 2 + (weights,) * 3,
        out_specs=tokens,
        check_vma=False,
    )
```

```python
import jax
import jax.numpy as jnp
from jax import lax
from jax.experimental import pallas as pl
from jax.experimental.pallas import tpu as pltpu
from jax.sharding import PartitionSpec as P

F32 = jnp.float32
BF16 = jnp.bfloat16
EXACT = lax.Precision.HIGHEST
VMEM_LIMIT = 24 * 1024 * 1024
PIECES = 3
LOG_ROWS = 32

VMEM_SPEC = pl.BlockSpec(memory_space=pltpu.VMEM)
SMEM_SPEC = pl.BlockSpec(memory_space=pltpu.SMEM)


def near(x):
    return pltpu.with_memory_space_constraint(x, pltpu.VMEM)


def far(x):
    return pltpu.with_memory_space_constraint(x, pltpu.HBM)


def local(body, name, outs, *args, scalars=(), scratch=()):
    made = pl.pallas_call(
        body,
        out_shape=tuple(pltpu.VMEM(shape, dtype) for shape, dtype in outs),
        grid_spec=pltpu.PrefetchScalarGridSpec(
            num_scalar_prefetch=len(scalars),
            grid=(1,),
            in_specs=[VMEM_SPEC] * len(args),
            out_specs=tuple(VMEM_SPEC for _ in outs),
            scratch_shapes=list(scratch),
        ),
        compiler_params=pltpu.CompilerParams(vmem_limit_bytes=VMEM_LIMIT),
        name=name,
    )(*scalars, *(near(a) for a in args))
    return made[0] if len(outs) == 1 else made


def dot(a, b, ca=1, cb=0, precision=None):
    return lax.dot_general(
        a, b, (((ca,), (cb,)), ((), ())), precision=precision, preferred_element_type=F32
    )


def iota(shape, dim):
    return lax.broadcasted_iota(jnp.int32, shape, dim)


def log_rows(logs, dh):
    row = iota((LOG_ROWS, dh), 0)
    out = jnp.zeros((LOG_ROWS, dh), F32)
    for i, rest in enumerate(logs):
        for piece in range(PIECES):
            part = rest.astype(BF16).astype(F32)
            out = jnp.where(row == PIECES * i + piece, part, out)
            rest = rest - part
    return out.astype(BF16)


def log_of(ref, i):
    first = ref.shape[0] - LOG_ROWS + PIECES * i
    a, b, c = (ref[first + p : first + p + 1, :].astype(F32) for p in range(PIECES))
    return a + b + c


def contrib_body(half_ref, k_ref, v_ref, decay_ref, out_ref, decayed_ref):
    heads, block = decay_ref.shape
    steps = pl.num_programs(0)
    dh = out_ref.shape[1]
    per = k_ref.shape[1] // dh
    step = pl.program_id(0)

    @pl.when(step == 0)
    def _():
        lower = (iota((block, block), 0) >= iota((block, block), 1)).astype(F32)
        cum = -dot(lower, decay_ref[...], 1, 1, precision=EXACT)
        total = cum[block - 1 : block, :]
        decayed_ref[...] = jnp.exp(total - cum)
        logs = [jnp.broadcast_to(total[:, h : h + 1], (1, dh)) for h in range(heads)]
        out_ref[heads * dh :, :] = log_rows(logs, dh)

    for i in range(per):
        cols = slice(i * dh, (i + 1) * dh)
        weight = decayed_ref[:, i : i + 1]
        for later in range(per, heads, per):
            weight = jnp.where(step == later // per, decayed_ref[:, later + i : later + i + 1], weight)
        kw = (k_ref[:, cols].astype(F32) * weight).astype(BF16)
        rows = pl.ds(pl.multiple_of((step * per + i) * dh, dh), dh)
        out_ref[rows, :] = dot(kw, v_ref[:, cols], 0, 0).astype(BF16)


def pair_body(core_ref, own_ref, other_ref, out_ref):
    dh = own_ref.shape[1]
    heads = (own_ref.shape[0] - LOG_ROWS) // dh
    is_even = core_ref[0] == 0
    logs = []
    for h in range(heads):
        rows = slice(h * dh, (h + 1) * dh)
        own, other = own_ref[rows, :].astype(F32), other_ref[rows, :].astype(F32)
        own_log, other_log = log_of(own_ref, h), log_of(other_ref, h)
        even, odd = jnp.where(is_even, own, other), jnp.where(is_even, other, own)
        out_ref[rows, :] = (jnp.exp(jnp.where(is_even, other_log, own_log)) * even + odd).astype(BF16)
        logs.append(own_log + other_log)
    out_ref[heads * dh :, :] = log_rows(logs, dh)


def carry_body(core_ref, chip_ref, own_ref, other_ref, *refs):
    *earlier, keep_ref, send_ref = refs
    dh = own_ref.shape[1]
    heads = keep_ref.shape[0] // dh
    is_even = core_ref[0] == 0
    chip = chip_ref[0]
    for h in range(heads):
        rows = slice(h * dh, (h + 1) * dh)
        state = jnp.zeros((dh, dh), F32)
        for back in range(len(earlier), 0, -1):
            ref = earlier[back - 1]
            joined = jnp.exp(log_of(ref, h)) * state + ref[rows, :].astype(F32)
            state = jnp.where(chip >= back, joined, 0.0)
        even = jnp.where(is_even, own_ref[rows, :].astype(F32), other_ref[rows, :].astype(F32))
        even_log = jnp.where(is_even, log_of(own_ref, h), log_of(other_ref, h))
        after = jnp.exp(even_log) * state + even
        keep_ref[rows, :] = jnp.where(is_even, state, after).astype(BF16)
        send_ref[rows, :] = jnp.where(is_even, after, state).astype(BF16)


def intra_body(q_ref, k_ref, v_ref, decay_ref, out_ref, grow_ref):
    heads, block = decay_ref.shape
    dh = q_ref.shape[1] // heads
    half = block // 2
    lower = (iota((block, block), 0) >= iota((block, block), 1)).astype(F32)
    decay = decay_ref[...]
    cum = -dot(lower, decay, 1, 1, precision=EXACT)
    cum_t = -dot(decay, lower, 1, 1, precision=EXACT)
    part = pl.program_id(0)
    grow_ref[part] = jnp.exp(cum)
    for h in range(heads):
        cols = slice(h * dh, (h + 1) * dh)
        for lo, hi in ((0, half), (half, block)):
            scores = dot(q_ref[lo:hi, cols], k_ref[:hi, cols], 1, 1)
            gap = cum[lo:hi, h : h + 1] - cum_t[h : h + 1, :hi]
            seen = iota((hi - lo, hi), 0) + lo >= iota((hi - lo, hi), 1)
            probs = jnp.where(seen, scores * jnp.exp(jnp.minimum(gap, 0.0)), 0.0).astype(BF16)
            out_ref[part, lo:hi, cols] = dot(probs, v_ref[:hi, cols])


def route_body(ids_ref, levels_ref, pick_ref, mix_ref, *, cap):
    slots, block = pick_ref.shape
    experts = slots // cap
    expert = iota((experts, block), 0)
    first = ids_ref[0:1, :] == expert
    second = ids_ref[1:2, :] == expert
    member = (first | second).astype(F32)
    earlier = (iota((block, block), 0) < iota((block, block), 1)).astype(BF16)
    rank = ((dot(member.astype(BF16), earlier) + 1.0) * member).astype(BF16)
    level = jnp.where(first, levels_ref[0:1, :], 0) + jnp.where(second, levels_ref[1:2, :], 0)
    level = level.astype(F32).astype(BF16)
    spread = (iota((slots, experts), 0) // cap == iota((slots, experts), 1)).astype(BF16)
    pick_ref[...] = (dot(spread, rank) == (iota((slots, block), 0) % cap + 1).astype(F32)).astype(BF16)
    spread = (iota((experts, slots), 1) // cap == iota((experts, slots), 0)).astype(BF16)
    used = dot(rank, spread, 0, 0) == (iota((block, slots), 1) % cap + 1).astype(F32)
    mix_ref[...] = jnp.where(used, dot(level, spread, 0, 0) * (1.0 / 256.0), 0.0).astype(BF16)


def some_heads(half, intra_ref, q_ref, state_ref, grow_ref, x_ref, gain_ref, h_ref, squares_ref):
    heads = grow_ref.shape[2]
    block, width = h_ref.shape
    dh = width // heads
    grow = grow_ref[half]
    squares = jnp.zeros((block, dh), F32)
    for h in range(heads):
        cols = slice(h * dh, (h + 1) * dh)
        all_cols = pl.ds(pl.multiple_of(half * width + h * dh, dh), dh)
        raw = intra_ref[half, :, cols] + grow[:, h : h + 1] * dot(q_ref[:, all_cols], state_ref[cols, :])
        scale = lax.rsqrt(jnp.mean(raw * raw, axis=-1, keepdims=True) + 1e-06)
        res = x_ref[:, all_cols].astype(F32) + gain_ref[:, all_cols] * (raw * scale)
        h_ref[:, cols] = res
        squares = squares + res * res
    squares_ref[...] = squares


def heads_body(half_ref, *refs):
    some_heads(half_ref[0], *refs)


def finish_body(
    core_ref, intra_ref, q_ref, got_ref, grow_ref, x_ref, attn_gain_ref, norm_gain_ref, pick_ref, own_ref, squares_ref,
    h_ref, send_ref, rest_ref, more_ref
):
    block, width = h_ref.shape
    half = width // 2
    core = core_ref[0]
    some_heads(1 - core, intra_ref, q_ref, got_ref, grow_ref, x_ref, attn_gain_ref, rest_ref, more_ref)
    squares = squares_ref[...] + more_ref[...]
    scale = lax.rsqrt(jnp.sum(squares, axis=-1, keepdims=True) / width + 1e-06)
    step = 512
    for c in range(0, width, step):
        cols = slice(c, c + step)
        from_half = slice(c % half, c % half + step)
        is_own = core == c // half
        res = jnp.where(is_own, own_ref[:, from_half], rest_ref[:, from_half])
        h_ref[:, cols] = res
        normed = (norm_gain_ref[:, cols] * res * scale).astype(BF16)
        send_ref[:, cols] = dot(pick_ref[...], normed).astype(BF16)


def expert_body(x_ref, gate_ref, up_ref, down_ref, out_ref, act_ref):
    hidden, width = down_ref.shape
    step = 256
    for c in range(0, hidden, step):
        cols = slice(c, c + step)
        gate = dot(x_ref[...], gate_ref[:, cols])
        up = dot(x_ref[...], up_ref[:, cols])
        act_ref[:, cols] = (gate / (1.0 + jnp.exp(-gate)) * up).astype(BF16)
    for c in range(0, width, step):
        cols = slice(c, c + step)
        out_ref[:, cols] = dot(act_ref[...], down_ref[:, cols]).astype(BF16)


def combine_body(back_ref, h_ref, mix_ref, out_ref, buf, sems):
    parts, _, step = buf.shape
    stores = []
    for i in range(parts):
        cols = slice(i * step, (i + 1) * step)
        buf[i] = (h_ref[:, cols] + dot(mix_ref[...], back_ref[:, cols])).astype(BF16)
        stores.append(pltpu.make_async_copy(buf.at[i], out_ref.at[:, cols], sems.at[i]))
        stores[i].start()
    for store in stores:
        store.wait()


def combine(back, h_res, mix):
    block, width = h_res.shape
    parts = 4
    return pl.pallas_call(
        combine_body,
        out_shape=jax.ShapeDtypeStruct((block, width), BF16),
        in_specs=[VMEM_SPEC] * 3,
        out_specs=pl.BlockSpec(memory_space=pltpu.HBM),
        scratch_shapes=[pltpu.VMEM((parts, block, width // parts), BF16), pltpu.SemaphoreType.DMA((parts,))],
        compiler_params=pltpu.CompilerParams(vmem_limit_bytes=VMEM_LIMIT),
        name="combine",
    )(near(back), near(h_res), near(mix))


def contribution(half, k, v, decay_t, steps=1):
    heads, block = decay_t.shape
    width = k.shape[1]
    dh = width // heads
    columns = pl.BlockSpec((block, width // 2 // steps), lambda i, half: (0, half[0] * steps + i))
    return pl.pallas_call(
        contrib_body,
        out_shape=pltpu.VMEM((width // 2 + LOG_ROWS, dh), BF16),
        grid_spec=pltpu.PrefetchScalarGridSpec(
            num_scalar_prefetch=1,
            grid=(steps,),
            in_specs=[columns, columns, pl.BlockSpec((heads // 2, block), lambda i, half: (half[0], 0))],
            out_specs=VMEM_SPEC,
            scratch_shapes=[pltpu.VMEM((block, heads // 2), F32)],
        ),
        compiler_params=pltpu.CompilerParams(vmem_limit_bytes=VMEM_LIMIT),
        name="contrib",
    )(half, far(k), far(v), far(decay_t))


def inside_block(q, k, v, decay_t):
    heads, block = decay_t.shape
    width = q.shape[1]
    columns = pl.BlockSpec((block, width // 2), lambda i: (0, i))
    return pl.pallas_call(
        intra_body,
        out_shape=(pltpu.VMEM((2, block, width // 2), F32), pltpu.VMEM((2, block, heads // 2), F32)),
        grid=(2,),
        in_specs=[columns, columns, columns, pl.BlockSpec((heads // 2, block), lambda i: (i, 0))],
        out_specs=(VMEM_SPEC, VMEM_SPEC),
        compiler_params=pltpu.CompilerParams(vmem_limit_bytes=VMEM_LIMIT),
        name="intra",
    )(far(q), far(k), far(v), far(decay_t))


def pair_states(k, v, decay_t, core):
    swap = [(i, i ^ 1) for i in range(lax.axis_size("seq"))]
    other = lax.ppermute(contribution(1 - core, k, v, decay_t), "seq", swap)
    own = contribution(core, k, v, decay_t)
    return own, other, local(pair_body, "pair", [(own.shape, BF16)], own, other, scalars=(core,))


def of_earlier_chips(pair):
    blocks = lax.axis_size("seq")
    chips = blocks // 2
    return {
        by: lax.ppermute(pair, "seq", [(i, (i // 2 + by) % chips * 2 + i % 2) for i in range(blocks)])
        for by in sorted(range(1, chips), key=lambda by: min(by, chips - by))
    }


def carried_states(own, other, earlier, core, chip):
    swap = [(i, i ^ 1) for i in range(lax.axis_size("seq"))]
    half = ((own.shape[0] - LOG_ROWS, own.shape[1]), BF16)
    keep, send = local(carry_body, "carry", [half, half], own, other, *earlier, scalars=(core, chip))
    return keep, lax.ppermute(send, "seq", swap)


def per_device(
    layer_input, queries, keys_in, values_in, decay_rate, attn_gain, norm_gain, expert_ids, gate_levels, w_gate, w_up, w_down
):
    x, q, k, v, decay_t = layer_input[0], queries[0], keys_in[0], values_in[0], decay_rate[0].T
    block, width = x.shape
    heads = decay_t.shape[0]
    experts = lax.axis_size("exp")
    cap = 3 * block // experts
    slots = experts * cap
    hidden = w_gate.shape[2]
    index = lax.axis_index("seq").reshape(1)
    core, chip = index & 1, index >> 1

    own, other, pair = pair_states(k, v, decay_t, core)
    pair, q, ids = lax.optimization_barrier((pair, q, expert_ids[0]))
    earlier = of_earlier_chips(pair)
    intra, grow = inside_block(q, k, v, decay_t)
    pick, mix = local(
        lambda *refs: route_body(*refs, cap=cap),
        "route",
        [((slots, block), BF16), ((block, slots), BF16)],
        ids.T,
        gate_levels[0].T,
    )
    *states, intra, grow, pick, mix = lax.optimization_barrier((*earlier.values(), intra, grow, pick, mix))
    earlier = dict(zip(earlier, states))
    keep, got = carried_states(own, other, [earlier[by] for by in sorted(earlier)], core, chip)
    common = (grow, x, attn_gain[None])
    half = (block, width // 2)
    per_row = (block, width // heads)
    own_res, squares = local(
        heads_body, "heads", [(half, F32), (per_row, F32)], intra, q, keep, *common, scalars=(core,)
    )
    h_res, send = local(
        finish_body,
        "finish",
        [((block, width), F32), ((slots, width), BF16)],
        *(intra, q, got, *common, norm_gain[None], pick, own_res, squares),
        scalars=(core,),
        scratch=[pltpu.VMEM(half, F32), pltpu.VMEM(per_row, F32)],
    )
    arrived = lax.all_to_all(send.reshape(experts, cap, width), "exp", 0, 0, tiled=True)
    done = local(
        expert_body,
        "expert",
        [((slots, width), BF16)],
        *(arrived.reshape(slots, width), w_gate[0], w_up[0], w_down[0]),
        scratch=[pltpu.VMEM((slots, hidden), BF16)],
    )
    back = lax.all_to_all(done.reshape(experts, cap, width), "exp", 0, 0, tiled=True)
    return combine(back.reshape(slots, width), h_res, mix)[None]


def solution(mesh):
    tokens = P("exp", "seq", None)
    whole = P()
    weights = P("exp", None, None)
    return jax.shard_map(
        per_device,
        mesh=mesh,
        in_specs=(tokens,) * 5 + (whole,) * 2 + (tokens,) * 2 + (weights,) * 3,
        out_specs=tokens,
        check_vma=False,
    )
```

```python
import jax
import jax.numpy as jnp
from jax import lax
from jax.experimental import pallas as pl
from jax.experimental.pallas import tpu as pltpu
from jax.sharding import PartitionSpec as P

F32 = jnp.float32
BF16 = jnp.bfloat16
EXACT = lax.Precision.HIGHEST
VMEM_LIMIT = 24 * 1024 * 1024
PIECES = 3
LOG_ROWS = 32

VMEM_SPEC = pl.BlockSpec(memory_space=pltpu.VMEM)
SMEM_SPEC = pl.BlockSpec(memory_space=pltpu.SMEM)


def near(x):
    return pltpu.with_memory_space_constraint(x, pltpu.VMEM)


def far(x):
    return pltpu.with_memory_space_constraint(x, pltpu.HBM)


def local(body, name, outs, *args, scalars=(), scratch=()):
    made = pl.pallas_call(
        body,
        out_shape=tuple(pltpu.VMEM(shape, dtype) for shape, dtype in outs),
        grid_spec=pltpu.PrefetchScalarGridSpec(
            num_scalar_prefetch=len(scalars),
            grid=(1,),
            in_specs=[VMEM_SPEC] * len(args),
            out_specs=tuple(VMEM_SPEC for _ in outs),
            scratch_shapes=list(scratch),
        ),
        compiler_params=pltpu.CompilerParams(vmem_limit_bytes=VMEM_LIMIT),
        name=name,
    )(*scalars, *(near(a) for a in args))
    return made[0] if len(outs) == 1 else made


def dot(a, b, ca=1, cb=0, precision=None):
    return lax.dot_general(
        a, b, (((ca,), (cb,)), ((), ())), precision=precision, preferred_element_type=F32
    )


def iota(shape, dim):
    return lax.broadcasted_iota(jnp.int32, shape, dim)


def log_rows(logs, dh):
    row = iota((LOG_ROWS, dh), 0)
    out = jnp.zeros((LOG_ROWS, dh), F32)
    for i, rest in enumerate(logs):
        for piece in range(PIECES):
            part = rest.astype(BF16).astype(F32)
            out = jnp.where(row == PIECES * i + piece, part, out)
            rest = rest - part
    return out.astype(BF16)


def log_of(ref, i):
    first = ref.shape[0] - LOG_ROWS + PIECES * i
    a, b, c = (ref[first + p : first + p + 1, :].astype(F32) for p in range(PIECES))
    return a + b + c


def contrib_body(half_ref, k_ref, v_ref, decay_ref, out_ref, decayed_ref):
    heads, block = decay_ref.shape
    steps = pl.num_programs(0)
    dh = out_ref.shape[1]
    per = k_ref.shape[1] // dh
    step = pl.program_id(0)

    @pl.when(step == 0)
    def _():
        lower = (iota((block, block), 0) >= iota((block, block), 1)).astype(F32)
        cum = -dot(lower, decay_ref[...], 1, 1, precision=EXACT)
        total = cum[block - 1 : block, :]
        decayed_ref[...] = jnp.exp(total - cum)
        logs = [jnp.broadcast_to(total[:, h : h + 1], (1, dh)) for h in range(heads)]
        out_ref[heads * dh :, :] = log_rows(logs, dh)

    for i in range(per):
        cols = slice(i * dh, (i + 1) * dh)
        weight = decayed_ref[:, i : i + 1]
        for later in range(per, heads, per):
            weight = jnp.where(step == later // per, decayed_ref[:, later + i : later + i + 1], weight)
        kw = (k_ref[:, cols].astype(F32) * weight).astype(BF16)
        rows = pl.ds(pl.multiple_of((step * per + i) * dh, dh), dh)
        out_ref[rows, :] = dot(kw, v_ref[:, cols], 0, 0).astype(BF16)


def first_contrib_body(half_ref, k_ref, v_ref, decay_ref, all_k_ref, all_v_ref, out_ref, k_out, v_out, decayed_ref, sems):
    width = k_out.shape[1]
    cols = pl.ds(pl.multiple_of((1 - half_ref[0]) * width, 128), width)
    loads = [
        pltpu.make_async_copy(ref.at[:, cols], out, sems.at[i])
        for i, (ref, out) in enumerate(((all_k_ref, k_out), (all_v_ref, v_out)))
    ]
    for load in loads:
        load.start()
    contrib_body(half_ref, k_ref, v_ref, decay_ref, out_ref, decayed_ref)
    for load in loads:
        load.wait()


def second_contrib_body(half_ref, k_ref, v_ref, decay_ref, out_ref, decayed_ref):
    contrib_body(half_ref, k_ref, v_ref, decay_ref, out_ref, decayed_ref)


def pair_body(core_ref, own_ref, other_ref, out_ref):
    dh = own_ref.shape[1]
    heads = (own_ref.shape[0] - LOG_ROWS) // dh
    is_even = core_ref[0] == 0
    logs = []
    for h in range(heads):
        rows = slice(h * dh, (h + 1) * dh)
        own, other = own_ref[rows, :].astype(F32), other_ref[rows, :].astype(F32)
        own_log, other_log = log_of(own_ref, h), log_of(other_ref, h)
        even, odd = jnp.where(is_even, own, other), jnp.where(is_even, other, own)
        out_ref[rows, :] = (jnp.exp(jnp.where(is_even, other_log, own_log)) * even + odd).astype(BF16)
        logs.append(own_log + other_log)
    out_ref[heads * dh :, :] = log_rows(logs, dh)


def carry_body(core_ref, chip_ref, own_ref, other_ref, *refs):
    *earlier, keep_ref, send_ref = refs
    dh = own_ref.shape[1]
    heads = keep_ref.shape[0] // dh
    is_even = core_ref[0] == 0
    chip = chip_ref[0]
    for h in range(heads):
        rows = slice(h * dh, (h + 1) * dh)
        state = jnp.zeros((dh, dh), F32)
        for back in range(len(earlier), 0, -1):
            ref = earlier[back - 1]
            joined = jnp.exp(log_of(ref, h)) * state + ref[rows, :].astype(F32)
            state = jnp.where(chip >= back, joined, 0.0)
        even = jnp.where(is_even, own_ref[rows, :].astype(F32), other_ref[rows, :].astype(F32))
        even_log = jnp.where(is_even, log_of(own_ref, h), log_of(other_ref, h))
        after = jnp.exp(even_log) * state + even
        keep_ref[rows, :] = jnp.where(is_even, state, after).astype(BF16)
        send_ref[rows, :] = jnp.where(is_even, after, state).astype(BF16)


def intra_body(q_ref, k_ref, v_ref, decay_ref, out_ref, grow_ref):
    heads, block = decay_ref.shape
    dh = q_ref.shape[1] // heads
    half = block // 2
    lower = (iota((block, block), 0) >= iota((block, block), 1)).astype(F32)
    decay = decay_ref[...]
    cum = -dot(lower, decay, 1, 1, precision=EXACT)
    cum_t = -dot(decay, lower, 1, 1, precision=EXACT)
    part = pl.program_id(0)
    grow_ref[part] = jnp.exp(cum)
    for h in range(heads):
        cols = slice(h * dh, (h + 1) * dh)
        for lo, hi in ((0, half), (half, block)):
            scores = dot(q_ref[lo:hi, cols], k_ref[:hi, cols], 1, 1)
            gap = cum[lo:hi, h : h + 1] - cum_t[h : h + 1, :hi]
            seen = iota((hi - lo, hi), 0) + lo >= iota((hi - lo, hi), 1)
            probs = jnp.where(seen, scores * jnp.exp(jnp.minimum(gap, 0.0)), 0.0).astype(BF16)
            out_ref[part, lo:hi, cols] = dot(probs, v_ref[:hi, cols])


def route_body(ids_ref, levels_ref, pick_ref, mix_ref, *, cap):
    slots, block = pick_ref.shape
    experts = slots // cap
    expert = iota((experts, block), 0)
    first = ids_ref[0:1, :] == expert
    second = ids_ref[1:2, :] == expert
    member = (first | second).astype(F32)
    earlier = (iota((block, block), 0) < iota((block, block), 1)).astype(BF16)
    rank = ((dot(member.astype(BF16), earlier) + 1.0) * member).astype(BF16)
    level = jnp.where(first, levels_ref[0:1, :], 0) + jnp.where(second, levels_ref[1:2, :], 0)
    level = level.astype(F32).astype(BF16)
    spread = (iota((slots, experts), 0) // cap == iota((slots, experts), 1)).astype(BF16)
    pick_ref[...] = (dot(spread, rank) == (iota((slots, block), 0) % cap + 1).astype(F32)).astype(BF16)
    spread = (iota((experts, slots), 1) // cap == iota((experts, slots), 0)).astype(BF16)
    used = dot(rank, spread, 0, 0) == (iota((block, slots), 1) % cap + 1).astype(F32)
    mix_ref[...] = jnp.where(used, dot(level, spread, 0, 0) * (1.0 / 256.0), 0.0).astype(BF16)


def some_heads(half, intra_ref, q_ref, state_ref, grow_ref, x_ref, gain_ref, h_ref, squares_ref):
    heads = grow_ref.shape[2]
    block, width = h_ref.shape
    dh = width // heads
    grow = grow_ref[half]
    squares = jnp.zeros((block, dh), F32)
    for h in range(heads):
        cols = slice(h * dh, (h + 1) * dh)
        all_cols = pl.ds(pl.multiple_of(half * width + h * dh, dh), dh)
        raw = intra_ref[half, :, cols] + grow[:, h : h + 1] * dot(q_ref[:, all_cols], state_ref[cols, :])
        scale = lax.rsqrt(jnp.mean(raw * raw, axis=-1, keepdims=True) + 1e-06)
        res = x_ref[:, all_cols].astype(F32) + gain_ref[:, all_cols] * (raw * scale)
        h_ref[:, cols] = res
        squares = squares + res * res
    squares_ref[...] = squares


def heads_body(half_ref, *refs):
    some_heads(half_ref[0], *refs)


def finish_body(
    core_ref, intra_ref, q_ref, got_ref, grow_ref, x_ref, attn_gain_ref, norm_gain_ref, pick_ref, own_ref, squares_ref,
    h_ref, send_ref, rest_ref, more_ref
):
    block, width = h_ref.shape
    half = width // 2
    core = core_ref[0]
    some_heads(1 - core, intra_ref, q_ref, got_ref, grow_ref, x_ref, attn_gain_ref, rest_ref, more_ref)
    squares = squares_ref[...] + more_ref[...]
    scale = lax.rsqrt(jnp.sum(squares, axis=-1, keepdims=True) / width + 1e-06)
    step = 512
    for c in range(0, width, step):
        cols = slice(c, c + step)
        from_half = slice(c % half, c % half + step)
        is_own = core == c // half
        res = jnp.where(is_own, own_ref[:, from_half], rest_ref[:, from_half])
        h_ref[:, cols] = res
        normed = (norm_gain_ref[:, cols] * res * scale).astype(BF16)
        send_ref[:, cols] = dot(pick_ref[...], normed).astype(BF16)


def expert_body(x_ref, gate_ref, up_ref, down_ref, out_ref, act_ref):
    hidden, width = down_ref.shape
    step = 256
    for c in range(0, hidden, step):
        cols = slice(c, c + step)
        gate = dot(x_ref[...], gate_ref[:, cols])
        up = dot(x_ref[...], up_ref[:, cols])
        act_ref[:, cols] = (gate / (1.0 + jnp.exp(-gate)) * up).astype(BF16)
    for c in range(0, width, step):
        cols = slice(c, c + step)
        out_ref[:, cols] = dot(act_ref[...], down_ref[:, cols]).astype(BF16)


def combine_body(back_ref, h_ref, mix_ref, out_ref, buf, sems):
    parts, _, step = buf.shape
    stores = []
    for i in range(parts):
        cols = slice(i * step, (i + 1) * step)
        buf[i] = (h_ref[:, cols] + dot(mix_ref[...], back_ref[:, cols])).astype(BF16)
        stores.append(pltpu.make_async_copy(buf.at[i], out_ref.at[:, cols], sems.at[i]))
        stores[i].start()
    for store in stores:
        store.wait()


def combine(back, h_res, mix):
    block, width = h_res.shape
    parts = 4
    return pl.pallas_call(
        combine_body,
        out_shape=jax.ShapeDtypeStruct((block, width), BF16),
        in_specs=[VMEM_SPEC] * 3,
        out_specs=pl.BlockSpec(memory_space=pltpu.HBM),
        scratch_shapes=[pltpu.VMEM((parts, block, width // parts), BF16), pltpu.SemaphoreType.DMA((parts,))],
        compiler_params=pltpu.CompilerParams(vmem_limit_bytes=VMEM_LIMIT),
        name="combine",
    )(near(back), near(h_res), near(mix))


def contributions(core, k, v, decay_t):
    heads, block = decay_t.shape
    width = k.shape[1] // 2
    dh = width // (heads // 2)
    columns = pl.BlockSpec((block, width), lambda i, half: (0, half[0]))
    rates = pl.BlockSpec((heads // 2, block), lambda i, half: (half[0], 0))
    states = pltpu.VMEM((width + LOG_ROWS, dh), BF16)
    decayed = pltpu.VMEM((block, heads // 2), F32)
    in_hbm = pl.BlockSpec(memory_space=pltpu.HBM)
    params = pltpu.CompilerParams(vmem_limit_bytes=VMEM_LIMIT)
    kept = pltpu.VMEM((block, width), BF16)
    k, v, decay_t = far(k), far(v), far(decay_t)
    first, k_own, v_own = pl.pallas_call(
        first_contrib_body,
        out_shape=(states, kept, kept),
        grid_spec=pltpu.PrefetchScalarGridSpec(
            num_scalar_prefetch=1,
            grid=(1,),
            in_specs=[columns, columns, rates, in_hbm, in_hbm],
            out_specs=(VMEM_SPEC,) * 3,
            scratch_shapes=[decayed, pltpu.SemaphoreType.DMA((2,))],
        ),
        compiler_params=params,
        name="contrib",
    )(1 - core, k, v, decay_t, k, v)

    def second():
        return pl.pallas_call(
            second_contrib_body,
            out_shape=states,
            grid_spec=pltpu.PrefetchScalarGridSpec(
                num_scalar_prefetch=1,
                grid=(1,),
                in_specs=[VMEM_SPEC, VMEM_SPEC, rates],
                out_specs=VMEM_SPEC,
                scratch_shapes=[decayed],
            ),
            compiler_params=params,
            name="contrib",
        )(core, near(k_own), near(v_own), decay_t)

    return first, second


def inside_block(q, k, v, decay_t):
    heads, block = decay_t.shape
    width = q.shape[1]
    columns = pl.BlockSpec((block, width // 2), lambda i: (0, i))
    return pl.pallas_call(
        intra_body,
        out_shape=(pltpu.VMEM((2, block, width // 2), F32), pltpu.VMEM((2, block, heads // 2), F32)),
        grid=(2,),
        in_specs=[columns, columns, columns, pl.BlockSpec((heads // 2, block), lambda i: (i, 0))],
        out_specs=(VMEM_SPEC, VMEM_SPEC),
        compiler_params=pltpu.CompilerParams(vmem_limit_bytes=VMEM_LIMIT),
        name="intra",
    )(far(q), far(k), far(v), far(decay_t))


def pair_states(k, v, decay_t, core):
    swap = [(i, i ^ 1) for i in range(lax.axis_size("seq"))]
    first, second = contributions(core, k, v, decay_t)
    other = lax.ppermute(first, "seq", swap)
    own = second()
    return own, other, local(pair_body, "pair", [(own.shape, BF16)], own, other, scalars=(core,))


def of_earlier_chips(pair):
    blocks = lax.axis_size("seq")
    chips = blocks // 2
    return {
        by: lax.ppermute(pair, "seq", [(i, (i // 2 + by) % chips * 2 + i % 2) for i in range(blocks)])
        for by in sorted(range(1, chips), key=lambda by: (min(by, chips - by), -by))
    }


def carried_states(own, other, earlier, core, chip):
    swap = [(i, i ^ 1) for i in range(lax.axis_size("seq"))]
    half = ((own.shape[0] - LOG_ROWS, own.shape[1]), BF16)
    keep, send = local(carry_body, "carry", [half, half], own, other, *earlier, scalars=(core, chip))
    return keep, lax.ppermute(send, "seq", swap)


def per_device(
    layer_input, queries, keys_in, values_in, decay_rate, attn_gain, norm_gain, expert_ids, gate_levels, w_gate, w_up, w_down
):
    x, q, k, v, decay_t = layer_input[0], queries[0], keys_in[0], values_in[0], decay_rate[0].T
    block, width = x.shape
    heads = decay_t.shape[0]
    experts = lax.axis_size("exp")
    cap = 3 * block // experts
    slots = experts * cap
    hidden = w_gate.shape[2]
    index = lax.axis_index("seq").reshape(1)
    core, chip = index & 1, index >> 1

    own, other, pair = pair_states(k, v, decay_t, core)
    pair, q, ids = lax.optimization_barrier((pair, q, expert_ids[0]))
    earlier = of_earlier_chips(pair)
    intra, grow = inside_block(q, k, v, decay_t)
    pick, mix = local(
        lambda *refs: route_body(*refs, cap=cap),
        "route",
        [((slots, block), BF16), ((block, slots), BF16)],
        ids.T,
        gate_levels[0].T,
    )
    *states, intra, grow, pick, mix = lax.optimization_barrier((*earlier.values(), intra, grow, pick, mix))
    earlier = dict(zip(earlier, states))
    keep, got = carried_states(own, other, [earlier[by] for by in sorted(earlier)], core, chip)
    common = (grow, x, attn_gain[None])
    half = (block, width // 2)
    per_row = (block, width // heads)
    own_res, squares = local(
        heads_body, "heads", [(half, F32), (per_row, F32)], intra, q, keep, *common, scalars=(core,)
    )
    h_res, send = local(
        finish_body,
        "finish",
        [((block, width), F32), ((slots, width), BF16)],
        *(intra, q, got, *common, norm_gain[None], pick, own_res, squares),
        scalars=(core,),
        scratch=[pltpu.VMEM(half, F32), pltpu.VMEM(per_row, F32)],
    )
    arrived = lax.all_to_all(send.reshape(experts, cap, width), "exp", 0, 0, tiled=True)
    done = local(
        expert_body,
        "expert",
        [((slots, width), BF16)],
        *(arrived.reshape(slots, width), w_gate[0], w_up[0], w_down[0]),
        scratch=[pltpu.VMEM((slots, hidden), BF16)],
    )
    back = lax.all_to_all(done.reshape(experts, cap, width), "exp", 0, 0, tiled=True)
    return combine(back.reshape(slots, width), h_res, mix)[None]


def solution(mesh):
    tokens = P("exp", "seq", None)
    whole = P()
    weights = P("exp", None, None)
    return jax.shard_map(
        per_device,
        mesh=mesh,
        in_specs=(tokens,) * 5 + (whole,) * 2 + (tokens,) * 2 + (weights,) * 3,
        out_specs=tokens,
        check_vma=False,
    )
```
